32 devices in a mesh: row: 4 (over y, core), col: 8 (over z, x).
Axes of the slice: x: 2, y: 2, z: 4, core: 2. Of those that a mesh axis runs over, the one named last changes fastest.
Arguments:
- kernels: bfloat16 [6, 4096, 6144], P(None, 'col', 'row'), may hold values from -0.03125 to 0.03125
- history: bfloat16 [6, 6144, 256], P(None, ('row', 'col')), may hold values from -6 to 6
- incident: float32 [32, 128, 256], P(('row', 'col')), may hold values from -6 to 6
- owner: int32 [32], replicated, may hold values from 0 to 3, as said below
- tile_pairs: int32 [384, 2], P(('row', 'col')), may hold values from 0 to 31, as said below
- tile_values: bfloat16 [384, 128, 128], P(('row', 'col')), may hold values from -0.109375 to 0.109375
- tile_counts: int32 [32], P(('row', 'col')), may hold values from 1 to 12, as said below
Outputs:
- density: float32 [32, 128, 256], P(('row', 'col'))
The draws below stay inside these ranges and needn't reach their ends.
Inputs may be any that keep to these rules, and one draw needn't show every extreme that they name: `owner`: within each block of 4 consecutive clusters starting at a multiple of 4, the owners are all different. tile_pairs[t, 0] is the cluster whose slot is t // 12; for a target cluster k the sources of its slot are distinct clusters whose block (cluster // 4) is k // 4 - 1, k // 4 or k // 4 + 1, modulo 8. `tile_counts`: some device has all 12 slots live.
All inputs are finite; a program needn't handle non-finite values.
Results may differ from the reference program's by a relative error of at most 0.0012.
Values may be sent and summed in bfloat16 or wider, within the bound.
No kernel may reach another device: no remote copies, remote signals or barrier semaphores. Data moves between devices by JAX's collectives and lax.ppermute only.
A program may use at most 128 MiB of HBM per device.

```python
import jax
import jax.numpy as jnp
from jax import lax

LAGS = 6
CLUSTER = 128
COLUMNS = 256
TILE_DEV = 12
SWEEPS = 3
CLUSTERS = 32
TARGETS = 4096
SOURCES = 6144
N_ROW = 4
N_COL = 8


def owner_table(key):
    keys = jax.random.split(jax.random.fold_in(key, 11), N_COL)
    table = jax.vmap(lambda sub_key: jax.random.permutation(sub_key, N_ROW))(keys)
    return table.reshape(-1).astype(jnp.int32)


def draw_owner(key, part):
    return owner_table(key)


def draw_tile_pairs(key, part):
    owners = owner_table(key)
    clusters = jnp.arange(CLUSTERS, dtype=jnp.int32)
    slot_of = (owners * N_COL + clusters // N_ROW).astype(jnp.int32)
    cluster_of_slot = jnp.zeros((CLUSTERS,), jnp.int32).at[slot_of].set(clusters)
    keys = jax.random.split(jax.random.fold_in(key, 23), CLUSTERS)
    orders = jax.vmap(lambda sub_key: jax.random.permutation(sub_key, 3 * N_ROW))(keys)
    orders = orders[:, :TILE_DEV].astype(jnp.int32)
    blocks = cluster_of_slot // N_ROW
    first = (blocks + N_COL - 1) % N_COL * N_ROW
    chosen = (first[:, None] + orders) % CLUSTERS
    targets = jnp.repeat(cluster_of_slot, TILE_DEV)
    sources = chosen.reshape(-1)
    return jnp.stack([targets, sources], axis=1).astype(jnp.int32)


def draw_tile_counts(key, part):
    shifts = jax.random.randint(jax.random.fold_in(key, 31), (CLUSTERS,), 0, 4).astype(jnp.int32)
    counts = jnp.maximum(jnp.right_shift(jnp.full((CLUSTERS,), TILE_DEV, jnp.int32), shifts), 1)
    busiest = jax.random.randint(jax.random.fold_in(key, 37), (), 0, CLUSTERS)
    return counts.at[busiest].set(TILE_DEV).astype(jnp.int32)


def block_levels(rng, dims, pieces, smallest, largest):
    def one(dim, parts):
        draws = jax.random.uniform(jax.random.fold_in(jax.random.fold_in(rng, 6), dim), (parts,), jnp.float32, smallest / len(pieces), largest / len(pieces))
        return jnp.repeat(jnp.exp(draws), dims[dim] // parts).reshape((-1,) + (1,) * (len(dims) - dim - 1))

    factor_of = one(*pieces[0])
    for cut in pieces[1:]:
        factor_of = factor_of * one(*cut)
    return factor_of


def noise(own_key, shape, spread, bound, cuts=(), kind=jnp.bfloat16):
    entries = jax.random.normal(own_key, shape, jnp.float32) * spread
    if len(cuts) > 0:
        entries = block_levels(own_key, shape, cuts, -0.22, 0.18) * entries
    return jnp.clip(entries, min=-bound, max=bound).astype(kind)


def setup_inputs(seed: int = 0) -> dict:
    seeds = jax.random.split(jax.random.key(seed), 8)
    kernels = noise(seeds[0], (LAGS, TARGETS, SOURCES), (LAGS * SOURCES) ** -0.5, 0.03125, ((1, 8), (2, 4)))
    history = noise(seeds[1], (LAGS, SOURCES, COLUMNS), 1.0, 6.0, ((1, 32),))
    incident = noise(seeds[2], (CLUSTERS, CLUSTER, COLUMNS), 1.0, 6.0, ((0, 32),), jnp.float32)
    owner = draw_owner(jax.random.fold_in(seeds[7], 71), 0)
    tile_pairs = draw_tile_pairs(jax.random.fold_in(seeds[7], 71), 0)
    tile_values = noise(seeds[5], (CLUSTERS * TILE_DEV, CLUSTER, CLUSTER), (2 * CLUSTER * TILE_DEV) ** -0.5, 0.109375, ((0, 32),))
    tile_counts = draw_tile_counts(jax.random.fold_in(seeds[7], 71), 0)
    return {"kernels": kernels, "history": history, "incident": incident, "owner": owner, "tile_pairs": tile_pairs, "tile_values": tile_values, "tile_counts": tile_counts}


damping = 0.7


def reference(kernels, history, incident, owner, tile_pairs, tile_values, tile_counts):
    retarded = jnp.zeros((TARGETS, COLUMNS), jnp.float32)
    for lag_step in range(LAGS):
        retarded = retarded + jnp.dot(kernels[lag_step], history[lag_step], preferred_element_type=jnp.float32)
    clusters = jnp.arange(CLUSTERS, dtype=jnp.int32)
    slot_of = (owner * N_COL + clusters // N_ROW).astype(jnp.int32)
    by_cluster = retarded.reshape(CLUSTERS, CLUSTER, COLUMNS)
    by_slot = jnp.zeros_like(by_cluster).at[slot_of].set(by_cluster)
    driven = incident - by_slot
    targets = tile_pairs[:, 0]
    sources = tile_pairs[:, 1]
    tgt_slot = (owner[targets] * N_COL + targets // N_ROW).astype(jnp.int32)
    src_slot = (owner[sources] * N_COL + sources // N_ROW).astype(jnp.int32)
    tile_index = jnp.arange(CLUSTERS * TILE_DEV, dtype=jnp.int32)
    holder = tile_index // TILE_DEV
    active = (tile_index % TILE_DEV < tile_counts[holder]) & (tgt_slot == holder)
    tiles_all = tile_values.reshape(CLUSTERS, TILE_DEV, CLUSTER, CLUSTER)
    slots_all = src_slot.reshape(CLUSTERS, TILE_DEV)
    flags_all = active.reshape(CLUSTERS, TILE_DEV)
    density = driven
    for sweep_step in range(SWEEPS):
        rounded = density.astype(jnp.bfloat16)

        def one_slot(inputs):
            tiles, slots, flags = inputs
            picked = jnp.where(flags[:, None, None], rounded[slots], jnp.zeros((), jnp.bfloat16))
            return lax.dot_general(tiles.astype(jnp.float32), picked.astype(jnp.float32), (((0, 2), (0, 1)), ((), ())))

        near_term = lax.map(one_slot, (tiles_all, slots_all, flags_all))
        density = density + damping * (driven - density - near_term)
    return density
```

```python
import functools

import jax
import jax.numpy as jnp
from jax import lax
from jax.experimental import pallas as pl
from jax.experimental.pallas import tpu as pltpu
from jax.sharding import PartitionSpec as P

SWEEPS = 3
CHUNKS = 1


damping = 0.7


def cost(flops, moved):
    return pl.CostEstimate(flops=flops, bytes_accessed=moved, transcendentals=0)


def dense_tiles(pick, live, tile_values):
    slots = pick.shape[0]
    _, rows, depth = tile_values.shape

    def body(pick_ref, live_ref, tile_ref, out_ref):
        keep = live_ref[pl.program_id(0)] > 0
        out_ref[...] = jnp.where(keep, tile_ref[0], jnp.zeros((), tile_ref.dtype))

    return pl.pallas_call(
        body,
        out_shape=jax.ShapeDtypeStruct((rows, slots * depth), tile_values.dtype),
        grid_spec=pltpu.PrefetchScalarGridSpec(
            num_scalar_prefetch=2,
            grid=(slots,),
            in_specs=[pl.BlockSpec((1, rows, depth), lambda q, pick, live: (pick[q], 0, 0))],
            out_specs=pl.BlockSpec((rows, depth), lambda q, pick, live: (0, q)),
        ),
        cost_estimate=cost(0, 4 * slots * rows * depth),
        name="dense_tiles",
    )(pick, live, tile_values)


def stack_rows(source, parts):
    count = len(parts)
    rows, width = parts[0].shape

    def body(source_ref, *refs):
        out_ref = refs[-1]
        wanted = source_ref[pl.program_id(0)]
        for m in range(count):

            @pl.when(wanted == m)
            def _(m=m):
                out_ref[...] = refs[m][...]

    return pl.pallas_call(
        body,
        out_shape=jax.ShapeDtypeStruct((count * rows, width), parts[0].dtype),
        grid_spec=pltpu.PrefetchScalarGridSpec(
            num_scalar_prefetch=1,
            grid=(count,),
            in_specs=[pl.BlockSpec((rows, width), lambda i, s: (0, 0))] * count,
            out_specs=pl.BlockSpec((rows, width), lambda i, s: (i, 0)),
        ),
        cost_estimate=cost(0, 4 * count * rows * width),
        name="stack_rows",
    )(source, *parts)


def multiply(where, kernels, sides, seed, inner, spread):
    lags, rows, _ = kernels.shape
    count = len(sides)
    _, depth, columns = sides[0][0].shape
    first = isinstance(seed, tuple)

    def body(where_ref, kernel_ref, seed_ref, *refs):
        blocks = refs[: 2 * count]
        if spread:
            outs, (total, pair, turned) = refs[2 * count : -3], refs[-3:]
        else:
            (total,), (pair,) = refs[2 * count : -1], refs[-1:]
        side, lag = pl.program_id(0), pl.program_id(1)

        @pl.when((side == 0) & (lag == 0))
        def _():
            if first:
                total[...] = jnp.zeros_like(total)
                height = seed_ref.shape[0]
                at = pl.multiple_of(where_ref[2] * height, height)
                total[pl.ds(at, height), :] = -seed_ref[...]
            else:
                total[...] = seed_ref[...]

        inside = where_ref[0]
        for s in range(count):

            @pl.when((side == s) & (where_ref[4 + 2 * s] > 0))
            def _(s=s):
                here = pl.multiple_of(inside * depth, depth)
                there = pl.multiple_of((1 - inside) * depth, depth)
                pair[pl.ds(here, depth), :] = blocks[2 * s][0]
                pair[pl.ds(there, depth), :] = blocks[2 * s + 1][0]
                total[...] += jnp.dot(kernel_ref[0], pair[...], preferred_element_type=jnp.float32)

        if spread:

            @pl.when((side == count - 1) & (lag == lags - 1))
            def _():
                turned[...] = total[...].T
                width = columns // spread
                for m in range(spread):
                    at = pl.multiple_of((where_ref[1] ^ m) * width, width)
                    outs[m][...] = turned[pl.ds(at, width), :]

    def block_map(s):
        return lambda p, j, w: (jnp.where(p == s, j * w[4 + 2 * s], 0 if s else (lags - 1) * w[4 + 2 * s]), 0, 0)

    block_specs = [pl.BlockSpec((1, depth, columns), block_map(s)) for s in range(count) for _ in range(2)]
    if first:
        seed, chunk = seed
        seed_spec = pl.BlockSpec((seed.shape[0], columns), lambda p, j, w: (0, chunk))
    else:
        seed_spec = pl.BlockSpec((rows, columns), lambda p, j, w: (0, 0))
    scratch = [pltpu.VMEM((2 * depth, columns), sides[0][0].dtype)]
    whole = (rows, columns)
    if spread:
        part = (columns // spread, rows)
        out_shape = [jax.ShapeDtypeStruct(part, jnp.float32)] * spread
        out_specs = [pl.BlockSpec(part, lambda p, j, w: (0, 0))] * spread
        scratch = [pltpu.VMEM(whole, jnp.float32)] + scratch + [pltpu.VMEM(whole[::-1], jnp.float32)]
    else:
        out_shape = jax.ShapeDtypeStruct(whole, jnp.float32)
        out_specs = pl.BlockSpec(whole, lambda p, j, w: (0, 0))

    return pl.pallas_call(
        body,
        out_shape=out_shape,
        grid_spec=pltpu.PrefetchScalarGridSpec(
            num_scalar_prefetch=1,
            grid=(count, lags),
            in_specs=[
                pl.BlockSpec((1, rows, 2 * depth), lambda p, j, w: (j * w[4 + 2 * p], 0, w[3 + 2 * p])),
                seed_spec,
                *block_specs,
            ],
            out_specs=out_specs,
            scratch_shapes=scratch,
        ),
        cost_estimate=cost(4 * count * lags * rows * depth * columns, 4 * count * lags * depth * (rows + columns)),
        name="multiply",
    )(where, kernels, seed, *[b for side in sides for b in side])


def multiply_plain(where, kernels, sides, seed, inner, spread):
    depth, columns = sides[0][0].shape[1:]
    rows = kernels.shape[1]
    if isinstance(seed, tuple):
        incident, chunk = seed
        total = jnp.zeros((rows, columns), jnp.float32)
        part = -lax.slice_in_dim(incident, chunk * columns, (chunk + 1) * columns, axis=1)
        total = lax.dynamic_update_slice_in_dim(total, part, where[2] * incident.shape[0], 0)
    else:
        total = seed
    for s, (own, other) in enumerate(sides):
        lower = jnp.where(where[0] == 0, own, other)
        upper = jnp.where(where[0] == 0, other, own)
        pair = jnp.concatenate([lower, upper], axis=1)
        piece = lax.dynamic_slice_in_dim(kernels, where[3 + 2 * s] * 2 * depth, 2 * depth, axis=2)
        product = lax.dot_general(piece, pair, (((0, 2), (0, 1)), ((), ())), preferred_element_type=jnp.float32)
        total = total + jnp.where(where[4 + 2 * s] > 0, product, jnp.zeros((), jnp.float32))
    if not spread:
        return total
    turned = total.T
    width = columns // spread
    return [lax.dynamic_slice_in_dim(turned, (where[1] ^ m) * width, width, 0) for m in range(spread)]


def sweep(chosen, dense, driven, density, rounded, left, right, last):
    width, rows = driven.shape
    count = chosen.shape[0]
    height = rows // count

    def body(chosen_ref, dense_ref, driven_ref, density_ref, rounded_ref, left_ref, right_ref, *outs):
        def term(ref, k):
            return lax.dot_general(
                ref[...],
                dense_ref[:, k * rows : (k + 1) * rows],
                (((1,), (1,)), ((), ())),
                preferred_element_type=jnp.float32,
            )

        near = term(rounded_ref, 1) + term(left_ref, 0) + term(right_ref, 2)
        old = density_ref[...]
        new = old + damping * (driven_ref[...] - old - near)
        if last:
            outs[-1][...] = new
            for m in range(count):
                at = pl.multiple_of(chosen_ref[m] * height, height)
                outs[m][...] = outs[-1][:, pl.ds(at, height)]
        else:
            outs[0][...] = new
            outs[1][...] = new.astype(outs[1].dtype)

    if last:
        out_shape = [jax.ShapeDtypeStruct((width, height), jnp.float32)] * count
        scratch = [pltpu.VMEM((width, rows), jnp.float32)]
    else:
        out_shape = [
            jax.ShapeDtypeStruct((width, rows), jnp.float32),
            jax.ShapeDtypeStruct((width, rows), rounded.dtype),
        ]
        scratch = []
    vmem = pl.BlockSpec(memory_space=pltpu.VMEM)
    return pl.pallas_call(
        body,
        out_shape=out_shape,
        in_specs=[pl.BlockSpec(memory_space=pltpu.SMEM)] + [vmem] * 6,
        out_specs=[vmem] * len(out_shape),
        scratch_shapes=scratch,
        cost_estimate=cost(6 * width * rows * rows, 6 * rows * rows + 20 * width * rows),
        name="sweep_last" if last else "sweep",
    )(chosen, dense, driven, density, rounded, left, right)


def assemble(place, groups):
    count = len(groups[0])
    width, height = groups[0][0].shape
    columns = len(groups) * count * width

    def body(place_ref, *refs):
        out_ref, turned = refs[-2:]
        for g in range(len(groups)):
            for m in range(count):
                at = pl.multiple_of((place_ref[1] ^ m) * width, width)
                turned[pl.ds(g * count * width + at, width), :] = refs[g * count + m][...]
        out_ref[0] = turned[...].T

    vmem = pl.BlockSpec(memory_space=pltpu.VMEM)
    flat = [piece for group in groups for piece in group]
    return pl.pallas_call(
        body,
        out_shape=jax.ShapeDtypeStruct((1, height, columns), jnp.float32),
        in_specs=[pl.BlockSpec(memory_space=pltpu.SMEM)] + [vmem] * len(flat),
        out_specs=vmem,
        scratch_shapes=[pltpu.VMEM((columns, height), jnp.float32)],
        cost_estimate=cost(0, 8 * columns * height),
        name="assemble",
    )(place, *flat)


def per_device(kernels, history, incident, owner, tile_pairs, tile_values, tile_counts):
    row_count = lax.axis_size("row")
    col_count = lax.axis_size("col")
    columns = history.shape[2]
    depth = history.shape[1]
    inner = 2
    outer = col_count // inner
    row_index = lax.axis_index("row")
    col_index = lax.axis_index("col")
    outer_at, inner_at = col_index // inner, col_index % inner

    def across_rows(x, m):
        return lax.ppermute(x, "row", [(i, i ^ m) for i in range(row_count)])

    def shifted(x, by):
        pairs = [(i, i + by * inner) for i in range(col_count) if 0 <= i + by * inner < col_count]
        return lax.ppermute(x, "col", pairs)

    def swapped(x, by):
        pairs = [(i ^ 1, i) for i in range(col_count) if 0 <= i // inner - by < outer]
        return lax.ppermute(x, "col", pairs)

    order = jnp.arange(row_count, dtype=jnp.int32)
    block_owner = lax.dynamic_slice_in_dim(owner, col_index * row_count, row_count)
    relative = order ^ row_index
    chosen = jnp.sum(jnp.where(block_owner[None, :] == relative[:, None], order[None, :], 0), axis=1)
    source_row = block_owner ^ row_index

    slots = jnp.arange(3 * row_count, dtype=jnp.int32)
    sources = tile_pairs[:, 1]
    window = (sources // row_count - col_index + 1 + col_count) % col_count * row_count + sources % row_count
    tiles = jnp.arange(tile_values.shape[0], dtype=jnp.int32)
    hit = (tiles < tile_counts[0])[None, :] & (window[None, :] == slots[:, None])
    pick = jnp.sum(jnp.where(hit, tiles[None, :], 0), axis=1)
    live = jnp.sum(hit.astype(jnp.int32), axis=1)
    own_tiles = dense_tiles(pick, live, tile_values)
    dense = stack_rows(source_row, [own_tiles] + [across_rows(own_tiles, m) for m in range(1, row_count)])

    product = multiply if (inner * depth) % 128 == 0 else multiply_plain

    def where_of(*sides):
        head = [inner_at, row_index, chosen[0]]
        for by in sides:
            at = outer_at - by
            there = (at >= 0) & (at < outer)
            head += [jnp.where(there, at, outer_at), there.astype(jnp.int32)]
        return jnp.stack([h.astype(jnp.int32) for h in head])

    place = where_of(0)
    width = columns // CHUNKS
    groups = []
    for chunk in range(CHUNKS):
        own = lax.slice_in_dim(history, chunk * width, (chunk + 1) * width, axis=2)
        low = high = own
        total = product(place, kernels, [(own, swapped(own, 0))], (incident[0], chunk), inner, 0)
        for step in range(1, outer):
            low, high = shifted(low, 1), shifted(high, -1)
            sides = [(low, swapped(low, step)), (high, swapped(high, -step))]
            spread = row_count if step == outer - 1 else 0
            total = product(where_of(step, -step), kernels, sides, total, inner, spread)
        summed = total[0]
        for m in range(1, row_count):
            summed = summed + across_rows(total[m], m)
        driven = -summed
        density = driven
        rounded = density.astype(jnp.bfloat16)
        for step in range(SWEEPS):
            left = lax.ppermute(rounded, "col", [(i, (i + 1) % col_count) for i in range(col_count)])
            right = lax.ppermute(rounded, "col", [((i + 1) % col_count, i) for i in range(col_count)])
            last = step == SWEEPS - 1
            result = sweep(chosen, dense, driven, density, rounded, left, right, last)
            if not last:
                density, rounded = result
        groups.append([result[0]] + [across_rows(result[m], m) for m in range(1, row_count)])
    return assemble(place, groups)


def solution(mesh):
    in_specs = (
        P(None, "col", "row"),
        P(None, ("row", "col"), None),
        P(("row", "col"), None, None),
        P(),
        P(("row", "col"), None),
        P(("row", "col"), None, None),
        P(("row", "col")),
    )
    out_specs = P(("row", "col"), None, None)
    return jax.shard_map(
        per_device, mesh=mesh, in_specs=in_specs, out_specs=out_specs, check_vma=False
    )
```

```python
import jax
import jax.numpy as jnp
from jax import lax
from jax.experimental import pallas as pl
from jax.experimental.pallas import tpu as pltpu
from jax.sharding import PartitionSpec as P

SWEEPS = 3
PARTS = 2
LANES = 128


damping = 0.7


def cost(flops, moved):
    return pl.CostEstimate(flops=flops, bytes_accessed=moved, transcendentals=0)


def params(limit):
    return pltpu.CompilerParams(vmem_limit_bytes=limit * 2**20)


VMEM = pl.BlockSpec(memory_space=pltpu.VMEM)
SMEM = pl.BlockSpec(memory_space=pltpu.SMEM)


def dense_tiles(pick, live, tile_values):
    slots = pick.shape[0]
    _, rows, depth = tile_values.shape

    def body(pick_ref, live_ref, tile_ref, out_ref):
        for q in range(slots):
            tile = tile_ref[pick_ref[q]]
            out_ref[:, q * depth : (q + 1) * depth] = jnp.where(live_ref[q] > 0, tile, jnp.zeros_like(tile))

    return pl.pallas_call(
        body,
        out_shape=jax.ShapeDtypeStruct((rows, slots * depth), tile_values.dtype),
        in_specs=[SMEM, SMEM, VMEM],
        out_specs=VMEM,
        compiler_params=params(8),
        cost_estimate=cost(0, 4 * slots * rows * depth),
        name="dense_tiles",
    )(pick, live, tile_values)


def stack_rows(chosen, parts):
    count = len(parts)
    rows, width = parts[0].shape

    def body(chosen_ref, *refs):
        for m in range(count):
            at = pl.multiple_of(chosen_ref[m] * rows, rows)
            refs[-1][pl.ds(at, rows), :] = refs[m][...]

    return pl.pallas_call(
        body,
        out_shape=jax.ShapeDtypeStruct((count * rows, width), parts[0].dtype),
        in_specs=[SMEM] + [VMEM] * count,
        out_specs=VMEM,
        compiler_params=params(16),
        cost_estimate=cost(0, 4 * count * rows * width),
        name="stack_rows",
    )(chosen, *parts)


def multiply(table, base, kernels, blocks, seed, spread):
    lags, rows, _ = kernels.shape
    lags //= PARTS
    count = len(blocks)
    places = (table.shape[0] - 2) // 2
    depth, columns = blocks[0][2].shape[1:]
    window = -(-(depth + LANES - 1) // LANES)
    tall = window * LANES
    first = seed.ndim == 2 and seed.shape[0] != rows
    order = [b[0] for b in blocks]
    part = [b[1] for b in blocks]
    whole_own = blocks[0][2].shape[0] != lags

    def body(table_ref, *refs):
        lanes, seed_ref = refs[:window], refs[window]
        given = refs[window + 1 : window + 1 + len(arrays)]
        rest = refs[window + 1 + len(arrays) :]
        if spread:
            keep, give, total, padded, turned = rest
        else:
            total, padded = rest
        step = pl.program_id(0)

        @pl.when(step == 0)
        def _():
            if first:
                total[...] = jnp.zeros_like(total)
                height = seed_ref.shape[0]
                at = pl.multiple_of(table_ref[2 * places + 1] * height, height)
                total[pl.ds(at, height), :] = -seed_ref[...]
            else:
                total[...] = seed_ref[...]

        padded[...] = jnp.zeros_like(padded)
        for s in range(count):

            @pl.when(step == s)
            def _(s=s):
                shift = table_ref[places + order[s]]
                source = given[0 if whole_own else s]
                for lag in range(lags):
                    at = pl.multiple_of(lag * tall + shift, 32)
                    padded[pl.ds(at, depth), :] = source[lag]

        left = jnp.concatenate([lanes[w][lag] for lag in range(lags) for w in range(window)], axis=1)
        total[...] += jnp.dot(left, padded[...], preferred_element_type=jnp.float32)

        if spread:

            @pl.when(step == count - 1)
            def _():
                turned[...] = total[...].T
                width = columns // spread
                for m in range(spread):
                    at = pl.multiple_of((table_ref[2 * places] ^ m) * width, width)
                    (give if m % 2 else keep)[m // 2] = turned[pl.ds(at, width), :]

    def static_pick(values, p):
        out = values[0]
        for s in range(1, len(values)):
            out = jnp.where(p == s, values[s], out)
        return out

    def lane_map(w):
        return lambda p, t: (static_pick(part, p), 0, t[static_pick(order, p)] + w)

    if whole_own:
        arrays = [blocks[0][2]]
        block_specs = [pl.BlockSpec((lags, depth, columns), lambda p, t: (p, 0, 0))]
    else:
        arrays = [b[2] for b in blocks]
        block_specs = [pl.BlockSpec((lags, depth, columns), lambda p, t: (0, 0, 0))] * count
    whole = (rows, columns)
    scratch = [pltpu.VMEM((lags * tall, columns), kernels.dtype)]
    if spread:
        piece = (spread // 2, columns // spread, rows)
        out_shape = [jax.ShapeDtypeStruct(piece, jnp.float32)] * 2
        out_specs = [pl.BlockSpec(piece, lambda p, t: (0, 0, 0))] * 2
        scratch = [pltpu.VMEM(whole, jnp.float32)] + scratch + [pltpu.VMEM(whole[::-1], jnp.float32)]
    else:
        out_shape = jax.ShapeDtypeStruct(whole, jnp.float32)
        out_specs = pl.BlockSpec(whole, lambda p, t: (0, 0))

    return pl.pallas_call(
        body,
        out_shape=out_shape,
        grid_spec=pltpu.PrefetchScalarGridSpec(
            num_scalar_prefetch=1,
            grid=(count,),
            in_specs=[pl.BlockSpec((lags, rows, LANES), lane_map(w)) for w in range(window)]
            + [pl.BlockSpec(seed.shape, lambda p, t: (0, 0))]
            + block_specs,
            out_specs=out_specs,
            scratch_shapes=scratch,
        ),
        compiler_params=params(24 if rows <= 512 else 56),
        cost_estimate=cost(2 * count * lags * rows * tall * columns, 2 * count * lags * tall * (rows + columns)),
        name="multiply",
    )(table, *[kernels] * window, seed, *arrays)


def sweep(chosen, dense, driven, density, rounded, left, right, last):
    width, rows = driven.shape
    count = chosen.shape[0]
    height = rows // count

    def body(chosen_ref, dense_ref, driven_ref, density_ref, rounded_ref, left_ref, right_ref, *outs):
        def term(ref, k):
            return lax.dot_general(
                ref[...],
                dense_ref[:, k * rows : (k + 1) * rows],
                (((1,), (1,)), ((), ())),
                preferred_element_type=jnp.float32,
            )

        near = term(rounded_ref, 1) + term(left_ref, 0) + term(right_ref, 2)
        old = density_ref[...]
        new = old + damping * (driven_ref[...] - old - near)
        if last:
            away, home, whole = outs
            whole[...] = new
            for m in range(count):
                at = pl.multiple_of(chosen_ref[m] * height, height)
                (away if m >= count // 2 else home)[m % (count // 2)] = whole[:, pl.ds(at, height)]
        else:
            outs[0][...] = new
            outs[1][...] = new.astype(outs[1].dtype)

    if last:
        out_shape = [jax.ShapeDtypeStruct((count // 2, width, height), jnp.float32)] * 2
        scratch = [pltpu.VMEM((width, rows), jnp.float32)]
    else:
        out_shape = [
            jax.ShapeDtypeStruct((width, rows), jnp.float32),
            jax.ShapeDtypeStruct((width, rows), rounded.dtype),
        ]
        scratch = []
    return pl.pallas_call(
        body,
        out_shape=out_shape,
        in_specs=[SMEM] + [VMEM] * 6,
        out_specs=[VMEM] * len(out_shape),
        scratch_shapes=scratch,
        compiler_params=params(24),
        cost_estimate=cost(6 * width * rows * rows, 6 * rows * rows + 20 * width * rows),
        name="sweep_last" if last else "sweep",
    )(chosen, dense, driven, density, rounded, left, right)


def assemble(table, pieces):
    arrays = [piece for _, piece in pieces]
    width, height = arrays[0].shape[1:]
    columns = width * sum(piece.shape[0] for piece in arrays)
    where = table.shape[0] - 2

    def body(table_ref, *refs):
        out_ref, turned = refs[-2:]
        for (offsets, _), ref in zip(pieces, refs):
            for t, m in enumerate(offsets):
                at = pl.multiple_of((table_ref[where] ^ m) * width, width)
                turned[pl.ds(at, width), :] = ref[t]
        out_ref[0] = turned[...].T

    return pl.pallas_call(
        body,
        out_shape=jax.ShapeDtypeStruct((1, height, columns), jnp.float32),
        in_specs=[SMEM] + [VMEM] * len(arrays),
        out_specs=VMEM,
        scratch_shapes=[pltpu.VMEM((columns, height), jnp.float32)],
        compiler_params=params(8),
        cost_estimate=cost(0, 8 * columns * height),
        name="assemble",
    )(table, *arrays)


def per_device(kernels, history, incident, owner, tile_pairs, tile_values, tile_counts):
    row_count = lax.axis_size("row")
    col_count = lax.axis_size("col")
    lags, depth, columns = history.shape
    half = lags // PARTS
    row_index = lax.axis_index("row")
    col_index = lax.axis_index("col")

    def across_rows(x, m):
        return lax.ppermute(x, "row", [(i, i ^ m) for i in range(row_count)])

    walk = list(range(0, col_count, 2)) + list(range(col_count - 1, 0, -2))

    def around(x, by):
        pairs = [(walk[p], walk[(p + by) % col_count]) for p in range(col_count)]
        return lax.ppermute(x, "col", pairs)

    places = [0] + [by for k in range(1, (col_count + 1) // 2) for by in (k, -k)] + [col_count // 2]
    spot = {by: k for k, by in enumerate(places)}
    count = len(places)
    own_spot = jnp.where(col_index % 2 == 0, col_index // 2, col_count - 1 - col_index // 2)
    index = jnp.arange(2 * count + 2, dtype=jnp.int32)
    k = index % count
    by = jnp.where(k % 2 == 1, (k + 1) // 2, -(k // 2))
    p = (own_spot - by + 2 * col_count) % col_count
    source = jnp.where(p < col_count // 2, 2 * p, 2 * (col_count - 1 - p) + 1)
    tall = -(-(depth + LANES - 1) // LANES)
    group = jnp.minimum(source * depth // LANES, kernels.shape[2] // LANES - tall)
    order = jnp.arange(row_count, dtype=jnp.int32)
    block_owner = lax.dynamic_slice_in_dim(owner, col_index * row_count, row_count)
    chosen = jnp.sum(
        jnp.where(block_owner[None, :] == (order ^ row_index)[:, None], order[None, :], 0), axis=1
    )
    table = jnp.where(index < count, group, source * depth - group * LANES)
    table = jnp.where(index == 2 * count, row_index, table)
    table = jnp.where(index == 2 * count + 1, jnp.sum(jnp.where(block_owner == row_index, order, 0)), table)

    slots = jnp.arange(3 * row_count, dtype=jnp.int32)
    sources = tile_pairs[:, 1]
    place = (sources // row_count - col_index + 1 + col_count) % col_count * row_count + sources % row_count
    tiles = jnp.arange(tile_values.shape[0], dtype=jnp.int32)
    hit = (tiles < tile_counts[0])[None, :] & (place[None, :] == slots[:, None])
    pick = jnp.sum(jnp.where(hit, tiles[None, :], 0), axis=1)
    live = jnp.sum(hit.astype(jnp.int32), axis=1)
    own_tiles = dense_tiles(pick, live, tile_values)
    dense = stack_rows(chosen, [own_tiles] + [across_rows(own_tiles, m) for m in range(1, row_count)])

    halves = [history[i * half : (i + 1) * half] for i in range(PARTS)]
    moving = {(way, i): halves[i] for i in range(PARTS) for way in (1, -1)}
    total = multiply(table, 0, kernels, [(0, i, history) for i in range(PARTS)], incident[0], 0)
    for step in range(1, (col_count + 1) // 2):
        moving = {key: around(x, key[0]) for key, x in moving.items()}
        blocks = [(spot[way * step], i, moving[way, i]) for i in range(PARTS) for way in (1, -1)]
        total = multiply(table, step, kernels, blocks, total, 0)
    far = spot[col_count // 2]
    blocks = [(far, i, around(moving[way, i], way)) for i, way in ((0, 1), (1, -1))]
    keep, give = multiply(table, far, kernels, blocks, total, row_count)

    bit = 1
    got = across_rows(give, bit)
    summed = [keep[t] + got[t] for t in range(row_count // 2)]
    while len(summed) > 1:
        bit *= 2
        odd = summed[1::2]
        got = across_rows(odd[0] if len(odd) == 1 else jnp.stack(odd), bit)
        got = [got] if len(odd) == 1 else [got[t] for t in range(len(odd))]
        summed = [a + b for a, b in zip(summed[0::2], got)]
    driven = -summed[0]

    density = driven
    rounded = density.astype(jnp.bfloat16)
    for step in range(SWEEPS):
        left = lax.ppermute(rounded, "col", [(i, (i + 1) % col_count) for i in range(col_count)])
        right = lax.ppermute(rounded, "col", [((i + 1) % col_count, i) for i in range(col_count)])
        result = sweep(chosen, dense, driven, density, rounded, left, right, step == SWEEPS - 1)
        if step < SWEEPS - 1:
            density, rounded = result

    away, home = result
    bit = row_count // 2
    got = across_rows(away, bit)
    sets = [((0,), home), ((bit,), got)]
    while bit > 1:
        bit //= 2
        pieces_next = []
        for offsets, array in sets:
            pieces_next.append((offsets, array[:bit]))
            sent = across_rows(array[bit : 2 * bit], bit)
            pieces_next.append((tuple(o ^ bit for o in offsets), sent))
        sets = pieces_next
    return assemble(table, [(offsets, array) for offsets, array in sets])


def solution(mesh):
    in_specs = (
        P(None, "col", "row"),
        P(None, ("row", "col"), None),
        P(("row", "col"), None, None),
        P(),
        P(("row", "col"), None),
        P(("row", "col"), None, None),
        P(("row", "col")),
    )
    out_specs = P(("row", "col"), None, None)
    return jax.shard_map(
        per_device, mesh=mesh, in_specs=in_specs, out_specs=out_specs, check_vma=False
    )
```

```python
import jax
import jax.numpy as jnp
from jax import lax
from jax.experimental import pallas as pl
from jax.experimental.pallas import tpu as pltpu
from jax.sharding import PartitionSpec as P


SWEEPS = 3
PARTS = 2
LANES = 128


damping = 0.7


def cost(flops, moved):
    return pl.CostEstimate(flops=flops, bytes_accessed=moved, transcendentals=0)


def params(limit):
    return pltpu.CompilerParams(vmem_limit_bytes=limit * 2**20)


VMEM = pl.BlockSpec(memory_space=pltpu.VMEM)
SMEM = pl.BlockSpec(memory_space=pltpu.SMEM)


def mate(p, side, count):
    return p ^ 1 if side == 1 else (p + (1 if p % 2 else -1)) % count


def early_side(step, part, final):
    return 1 if (final - step + part) % 2 == 0 else 2


def prepare(owner, pairs, counts, tile_values):
    rows = lax.axis_size("row")
    cols = lax.axis_size("col")
    tiles, height, deep = tile_values.shape
    slots = 3 * rows

    def body(owner_ref, pairs_ref, counts_ref, tile_ref, chosen_ref, out_ref, pick, live):
        row, col = lax.axis_index("row"), lax.axis_index("col")
        for i in range(rows):
            chosen_ref[owner_ref[col * rows + i] ^ row] = i
        for q in range(slots):
            pick[q] = 0
            live[q] = 0
        ahead = jnp.where(lax.rem(col, 2) == 0, 1, cols - 1)
        for t in range(tiles):

            @pl.when(t < counts_ref[0])
            def _(t=t):
                source = pairs_ref[1, t]
                apart = lax.rem(source // rows - col + cols, cols)
                block = jnp.where(apart == 0, 1, jnp.where(apart == ahead, 2, 0))
                slot = block * rows + lax.rem(source, rows)
                pick[slot] = t
                live[slot] = 1

        for q in range(slots):
            tile = tile_ref[pick[q]]
            out_ref[:, q * deep : (q + 1) * deep] = jnp.where(live[q] > 0, tile, jnp.zeros_like(tile))

    return pl.pallas_call(
        body,
        out_shape=[
            jax.ShapeDtypeStruct((rows,), jnp.int32),
            jax.ShapeDtypeStruct((height, slots * deep), tile_values.dtype),
        ],
        in_specs=[SMEM] * 3 + [VMEM],
        out_specs=[SMEM, VMEM],
        scratch_shapes=[pltpu.SMEM((slots,), jnp.int32), pltpu.SMEM((slots,), jnp.int32)],
        compiler_params=params(4),
        cost_estimate=cost(0, 4 * slots * height * deep),
        name="prepare",
    )(owner, pairs, counts, tile_values)


def stack_rows(chosen, parts):
    count = len(parts)
    rows, width = parts[0].shape

    def body(chosen_ref, *refs):
        for m in range(count):
            at = pl.multiple_of(chosen_ref[m] * rows, rows)
            refs[-1][pl.ds(at, rows), :] = refs[m][...]

    return pl.pallas_call(
        body,
        out_shape=jax.ShapeDtypeStruct((count * rows, width), parts[0].dtype),
        in_specs=[SMEM] + [VMEM] * count,
        out_specs=VMEM,
        compiler_params=params(4 if rows * count <= 512 else 24),
        cost_estimate=cost(0, 4 * count * rows * width),
        name="stack_rows",
    )(chosen, *parts)


def multiply(kernels, blocks, seed, incident, chosen, spread):
    rows = kernels.shape[1]
    cols = lax.axis_size("col")
    count = len(blocks)
    lags, depth, columns = blocks[0][3].shape
    tall = -(-(depth + LANES - 1) // LANES) * LANES
    extra = ([] if seed is None else [seed]) + ([] if incident is None else [incident, chosen])

    def body(kernel_ref, *refs):
        given, refs = refs[:count], refs[count:]
        seed_ref, refs = (None, refs) if seed is None else (refs[0], refs[1:])
        if incident is not None:
            (incident_ref, chosen_ref), refs = refs[:2], refs[2:]
        if spread:
            keep, give, (padded, total, turned) = refs[0], refs[1:-3], refs[-3:]
        else:
            total, padded = refs
        row, col = lax.axis_index("row"), lax.axis_index("col")
        stop = jnp.where(lax.rem(col, 2) == 0, col // 2, cols - 1 - col // 2)
        sign = jnp.where(lax.rem(stop, 2) == 1, 1, -1)
        padded[...] = jnp.zeros_like(padded)
        for s, (step, side, part, _) in enumerate(blocks):
            back = sign * (step if side == 1 else -step)
            at = lax.rem(stop - back + cols, cols)
            source = jnp.where(at < cols // 2, 2 * at, 2 * (cols - 1 - at) + 1)
            group = jnp.minimum(source * depth // LANES, (kernels.shape[2] - tall) // LANES)
            shift = source * depth - group * LANES
            for lag in range(lags):
                place = pl.multiple_of(lag * tall + shift, 32)
                padded[s, pl.ds(place, depth), :] = given[s][lag]
            lane = pl.multiple_of(group * LANES, LANES)
            left = jnp.concatenate([kernel_ref[part * lags + lag, :, pl.ds(lane, tall)] for lag in range(lags)], axis=1)
            product = jnp.dot(left, padded[s], preferred_element_type=jnp.float32)
            if s or seed is not None:
                product = (total if s else seed_ref)[...] + product
            total[...] = product
        if incident is not None:
            height = incident.shape[0]
            mine = pl.ds(pl.multiple_of(chosen_ref[0] * height, height), height)
            total[mine, :] = total[mine, :] - incident_ref[...]
        if spread:
            turned[...] = total[...].T
            width = columns // spread
            for m in range(spread):
                at = pl.multiple_of((row ^ m) * width, width)
                value = turned[pl.ds(at, width), :]
                if m % 2:
                    give[m // 2][...] = value
                else:
                    keep[m // 2] = value

    whole = (rows, columns)
    scratch = [pltpu.VMEM((count, lags * tall, columns), kernels.dtype)]
    if spread:
        piece = (columns // spread, rows)
        out_shape = [jax.ShapeDtypeStruct((spread // 2, *piece), jnp.float32)]
        out_shape += [jax.ShapeDtypeStruct(piece, jnp.float32)] * (spread // 2)
        scratch += [pltpu.VMEM(whole, jnp.float32), pltpu.VMEM(whole[::-1], jnp.float32)]
    else:
        out_shape = jax.ShapeDtypeStruct(whole, jnp.float32)
    in_specs = [VMEM] * (1 + count + len(extra))
    if incident is not None:
        in_specs[-1] = SMEM

    return pl.pallas_call(
        body,
        out_shape=out_shape,
        in_specs=in_specs,
        out_specs=[VMEM] * len(out_shape) if spread else VMEM,
        scratch_shapes=scratch,
        compiler_params=params(16 if rows <= 512 else 40),
        cost_estimate=cost(2 * count * lags * rows * tall * columns, 2 * count * lags * tall * (rows + columns)),
        name="multiply",
    )(kernels, *[block[3] for block in blocks], *extra)


def steady(dense, driven, density, rounded, near_side):
    width, rows = driven.shape

    def body(dense_ref, driven_ref, density_ref, rounded_ref, side_ref, out_ref):
        def term(ref, k):
            return lax.dot_general(
                ref[...],
                dense_ref[:, k * rows : (k + 1) * rows],
                (((1,), (1,)), ((), ())),
                preferred_element_type=jnp.float32,
            )

        near = term(rounded_ref, 1) + term(side_ref, 2)
        old = density_ref[...]
        out_ref[...] = old + damping * (driven_ref[...] - old - near)

    return pl.pallas_call(
        body,
        out_shape=jax.ShapeDtypeStruct((width, rows), jnp.float32),
        in_specs=[VMEM] * 5,
        out_specs=VMEM,
        compiler_params=params(8 if rows <= 512 else 24),
        cost_estimate=cost(4 * width * rows * rows, 4 * rows * rows + 16 * width * rows),
        name="steady",
    )(dense, driven, density, rounded, near_side)


def sweep(dense, base, far_side, chosen):
    width, rows = base.shape

    def update(dense_ref, base_ref, side_ref):
        near = lax.dot_general(
            side_ref[...], dense_ref[:, :rows], (((1,), (1,)), ((), ())), preferred_element_type=jnp.float32
        )
        return base_ref[...] - damping * near

    def body(dense_ref, base_ref, side_ref, density_ref, rounded_ref):
        new = update(dense_ref, base_ref, side_ref)
        density_ref[...] = new
        rounded_ref[...] = new.astype(rounded_ref.dtype)

    def body_last(chosen_ref, dense_ref, base_ref, side_ref, away, home, whole):
        whole[...] = update(dense_ref, base_ref, side_ref)
        for m in range(count):
            at = pl.multiple_of(chosen_ref[m] * height, height)
            (away if m >= count // 2 else home)[m % (count // 2)] = whole[:, pl.ds(at, height)]

    same = dict(
        out_specs=[VMEM] * 2,
        compiler_params=params(8 if rows <= 512 else 24),
        cost_estimate=cost(2 * width * rows * rows, 2 * rows * rows + 12 * width * rows),
    )
    if chosen is None:
        out_shape = [
            jax.ShapeDtypeStruct((width, rows), jnp.float32),
            jax.ShapeDtypeStruct((width, rows), far_side.dtype),
        ]
        return pl.pallas_call(body, out_shape=out_shape, in_specs=[VMEM] * 3, name="sweep", **same)(
            dense, base, far_side
        )
    count = chosen.shape[0]
    height = rows // count
    return pl.pallas_call(
        body_last,
        out_shape=[jax.ShapeDtypeStruct((count // 2, width, height), jnp.float32)] * 2,
        in_specs=[SMEM] + [VMEM] * 3,
        scratch_shapes=[pltpu.VMEM((width, rows), jnp.float32)],
        name="sweep_last",
        **same,
    )(chosen, dense, base, far_side)


def assemble(pieces):
    arrays = [piece for _, piece in pieces]
    width, height = arrays[0].shape[1:]
    columns = width * sum(piece.shape[0] for piece in arrays)

    def body(*refs):
        row = lax.axis_index("row")
        out_ref, turned = refs[-2:]
        for (offsets, _), ref in zip(pieces, refs):
            for t, m in enumerate(offsets):
                at = pl.multiple_of((row ^ m) * width, width)
                turned[pl.ds(at, width), :] = ref[t]
        out_ref[0] = turned[...].T

    return pl.pallas_call(
        body,
        out_shape=jax.ShapeDtypeStruct((1, height, columns), jnp.float32),
        in_specs=[VMEM] * len(arrays),
        out_specs=VMEM,
        scratch_shapes=[pltpu.VMEM((columns, height), jnp.float32)],
        compiler_params=params(8),
        cost_estimate=cost(0, 8 * columns * height),
        name="assemble",
    )(*arrays)


def per_device(kernels, history, incident, owner, tile_pairs, tile_values, tile_counts):
    row_count = lax.axis_size("row")
    col_count = lax.axis_size("col")
    lags, _, _ = history.shape
    half = lags // PARTS

    def across_rows(x, m):
        return lax.ppermute(x, "row", [(i, i ^ m) for i in range(row_count)])

    walk = list(range(0, col_count, 2)) + list(range(col_count - 1, 0, -2))

    def swap_walk(x, side):
        return lax.ppermute(x, "col", [(walk[p], walk[mate(p, side, col_count)]) for p in range(col_count)])

    def swap_cols(x, side):
        return lax.ppermute(x, "col", [(c, mate(c, side, col_count)) for c in range(col_count)])

    chosen, own_tiles = prepare(owner, tile_pairs.T, tile_counts, tile_values)
    parts = [own_tiles]
    for m in range(1, row_count):
        parts.append(across_rows(own_tiles, m))
    dense = stack_rows(chosen, parts)

    halves = [history[i * half : (i + 1) * half] for i in range(PARTS)]
    moving = {(side, i): halves[i] for i in range(PARTS) for side in (1, 2)}
    final = col_count // 2

    def turn(step, rank):
        out = {}
        for i in range(PARTS):
            side = early_side(step, i, final) if rank == 0 else 3 - early_side(step, i, final)
            out[side, i] = swap_walk(moving[3 - side, i], side)
        return out

    total = multiply(kernels, [(0, 1, i, x) for i, x in enumerate(halves)], None, None, None, 0)
    for step in range(1, final):
        turns = [turn(step, rank) for rank in range(2)]
        moving = turns[0] | turns[1]
        for rank in range(2):
            blocks = [(step, side, i, x) for (side, i), x in turns[rank].items()]
            field = (incident[0], chosen) if (step, rank) == (final - 1, 1) else (None, None)
            total = multiply(kernels, blocks, total, *field, 0)
    blocks = [(final, 1, i, x) for (_, i), x in turn(final, 0).items()]
    keep, *give = multiply(kernels, blocks, total, None, None, row_count)

    bit = 1
    summed = [keep[t] + across_rows(give[t], bit) for t in range(row_count // 2)]
    while len(summed) > 1:
        bit *= 2
        summed = [summed[t] + across_rows(summed[t + 1], bit) for t in range(0, len(summed), 2)]
    driven = -summed[0]

    density = driven
    rounded = density.astype(jnp.bfloat16)
    for step in range(SWEEPS):
        far_side, near_side = swap_cols(rounded, 2), swap_cols(rounded, 1)
        base = steady(dense, driven, density, rounded, near_side)
        result = sweep(dense, base, far_side, chosen if step == SWEEPS - 1 else None)
        if step < SWEEPS - 1:
            density, rounded = result

    away, home = result
    bit = row_count // 2
    got = across_rows(away, bit)
    sets = [((0,), home), ((bit,), got)]
    while bit > 1:
        bit //= 2
        pieces_next = []
        for offsets, array in sets:
            pieces_next.append((offsets, array[:bit]))
            sent = across_rows(array[bit : 2 * bit], bit)
            pieces_next.append((tuple(o ^ bit for o in offsets), sent))
        sets = pieces_next
    return assemble([(offsets, array) for offsets, array in sets])


def solution(mesh):
    in_specs = (
        P(None, "col", "row"),
        P(None, ("row", "col"), None),
        P(("row", "col"), None, None),
        P(),
        P(("row", "col"), None),
        P(("row", "col"), None, None),
        P(("row", "col")),
    )
    out_specs = P(("row", "col"), None, None)
    return jax.shard_map(
        per_device, mesh=mesh, in_specs=in_specs, out_specs=out_specs, check_vma=False
    )
```

```python
import jax
import jax.numpy as jnp
from jax import lax
from jax.experimental import pallas as pl
from jax.experimental.pallas import tpu as pltpu
from jax.sharding import PartitionSpec as P


SWEEPS = 3
PARTS = 2
LANES = 128


damping = 0.7


def cost(flops, moved):
    return pl.CostEstimate(flops=flops, bytes_accessed=moved, transcendentals=0)


def params(limit):
    return pltpu.CompilerParams(vmem_limit_bytes=limit * 2**20)


VMEM = pl.BlockSpec(memory_space=pltpu.VMEM)
SMEM = pl.BlockSpec(memory_space=pltpu.SMEM)


def mate(p, side, count):
    return p ^ 1 if side == 1 else (p + (1 if p % 2 else -1)) % count


def early_side(step, part, final):
    return 1 if (final - step + part) % 2 == 0 else 2


def prepare(owner, pairs, counts, tile_values):
    rows = lax.axis_size("row")
    cols = lax.axis_size("col")
    tiles, height, deep = tile_values.shape
    slots = 3 * rows

    def body(owner_ref, pairs_ref, counts_ref, tile_ref, chosen_ref, out_ref, pick, live):
        row, col = lax.axis_index("row"), lax.axis_index("col")
        for i in range(rows):
            chosen_ref[owner_ref[col * rows + i] ^ row] = i
        for q in range(slots):
            pick[q] = 0
            live[q] = 0
        ahead = jnp.where(lax.rem(col, 2) == 0, 1, cols - 1)
        for t in range(tiles):

            @pl.when(t < counts_ref[0])
            def _(t=t):
                source = pairs_ref[1, t]
                apart = lax.rem(source // rows - col + cols, cols)
                block = jnp.where(apart == 0, 1, jnp.where(apart == ahead, 2, 0))
                slot = block * rows + lax.rem(source, rows)
                pick[slot] = t
                live[slot] = 1

        for q in range(slots):
            tile = tile_ref[pick[q]]
            out_ref[:, q * deep : (q + 1) * deep] = jnp.where(live[q] > 0, tile, jnp.zeros_like(tile))

    return pl.pallas_call(
        body,
        out_shape=[
            jax.ShapeDtypeStruct((rows,), jnp.int32),
            jax.ShapeDtypeStruct((height, slots * deep), tile_values.dtype),
        ],
        in_specs=[SMEM] * 3 + [VMEM],
        out_specs=[SMEM, VMEM],
        scratch_shapes=[pltpu.SMEM((slots,), jnp.int32), pltpu.SMEM((slots,), jnp.int32)],
        compiler_params=params(4),
        cost_estimate=cost(0, 4 * slots * height * deep),
        name="prepare",
    )(owner, pairs, counts, tile_values)


def stack_rows(chosen, parts):
    count = len(parts)
    rows, width = parts[0].shape
    side = width // 3

    def body(chosen_ref, *refs):
        for m in range(count):
            at = pl.multiple_of(chosen_ref[m] * rows, rows)
            refs[-2][pl.ds(at, rows), :] = refs[m][...]
            refs[-1][m * rows : (m + 1) * rows, :] = refs[m][:, :side]

    return pl.pallas_call(
        body,
        out_shape=[
            jax.ShapeDtypeStruct((count * rows, width), parts[0].dtype),
            jax.ShapeDtypeStruct((count * rows, side), parts[0].dtype),
        ],
        in_specs=[SMEM] + [VMEM] * count,
        out_specs=[VMEM] * 2,
        compiler_params=params(4 if rows * count <= 512 else 24),
        cost_estimate=cost(0, 4 * count * rows * width),
        name="stack_rows",
    )(chosen, *parts)


def multiply(kernels, blocks, seed, incident, chosen, spread):
    rows = kernels.shape[1]
    cols = lax.axis_size("col")
    count = len(blocks)
    lags, depth, columns = blocks[0][3].shape
    tall = -(-(depth + LANES - 1) // LANES) * LANES
    extra = ([] if seed is None else [seed]) + ([] if incident is None else [incident, chosen])

    def body(kernel_ref, *refs):
        given, refs = refs[:count], refs[count:]
        seed_ref, refs = (None, refs) if seed is None else (refs[0], refs[1:])
        if incident is not None:
            (incident_ref, chosen_ref), refs = refs[:2], refs[2:]
        if spread:
            keep, give, (padded, total, turned) = refs[0], refs[1:-3], refs[-3:]
        else:
            total, padded = refs
        row, col = lax.axis_index("row"), lax.axis_index("col")
        stop = jnp.where(lax.rem(col, 2) == 0, col // 2, cols - 1 - col // 2)
        sign = jnp.where(lax.rem(stop, 2) == 1, 1, -1)
        padded[...] = jnp.zeros_like(padded)
        for s, (step, side, part, _) in enumerate(blocks):
            back = sign * (step if side == 1 else -step)
            at = lax.rem(stop - back + cols, cols)
            source = jnp.where(at < cols // 2, 2 * at, 2 * (cols - 1 - at) + 1)
            group = jnp.minimum(source * depth // LANES, (kernels.shape[2] - tall) // LANES)
            shift = source * depth - group * LANES
            for lag in range(lags):
                place = pl.multiple_of(lag * tall + shift, 32)
                padded[s, pl.ds(place, depth), :] = given[s][lag]
            lane = pl.multiple_of(group * LANES, LANES)
            left = jnp.concatenate([kernel_ref[part * lags + lag, :, pl.ds(lane, tall)] for lag in range(lags)], axis=1)
            product = jnp.dot(left, padded[s], preferred_element_type=jnp.float32)
            if s or seed is not None:
                product = (total if s else seed_ref)[...] + product
            total[...] = product
        if incident is not None:
            height = incident.shape[0]
            mine = pl.ds(pl.multiple_of(chosen_ref[0] * height, height), height)
            total[mine, :] = total[mine, :] - incident_ref[...]
        if spread:
            turned[...] = total[...].T
            width = columns // spread
            for m in range(spread):
                at = pl.multiple_of((row ^ m) * width, width)
                value = turned[pl.ds(at, width), :]
                if m % 2:
                    give[m // 2][...] = value
                else:
                    keep[m // 2] = value

    whole = (rows, columns)
    scratch = [pltpu.VMEM((count, lags * tall, columns), kernels.dtype)]
    if spread:
        piece = (columns // spread, rows)
        out_shape = [jax.ShapeDtypeStruct((spread // 2, *piece), jnp.float32)]
        out_shape += [jax.ShapeDtypeStruct(piece, jnp.float32)] * (spread // 2)
        scratch += [pltpu.VMEM(whole, jnp.float32), pltpu.VMEM(whole[::-1], jnp.float32)]
    else:
        out_shape = jax.ShapeDtypeStruct(whole, jnp.float32)
    in_specs = [VMEM] * (1 + count + len(extra))
    if incident is not None:
        in_specs[-1] = SMEM

    return pl.pallas_call(
        body,
        out_shape=out_shape,
        in_specs=in_specs,
        out_specs=[VMEM] * len(out_shape) if spread else VMEM,
        scratch_shapes=scratch,
        compiler_params=params(16 if rows <= 512 else 40),
        cost_estimate=cost(2 * count * lags * rows * tall * columns, 2 * count * lags * tall * (rows + columns)),
        name="multiply",
    )(kernels, *[block[3] for block in blocks], *extra)


def steady(dense, driven, density, rounded, near_side, chosen):
    width, rows = driven.shape

    def body(*refs):
        dense_ref, driven_ref, density_ref, rounded_ref, side_ref, out_ref = refs[:5] + refs[-1 if last else 5 :][:1]

        def term(ref, k):
            return lax.dot_general(
                ref[...],
                dense_ref[:, k * rows : (k + 1) * rows],
                (((1,), (1,)), ((), ())),
                preferred_element_type=jnp.float32,
            )

        near = term(rounded_ref, 1) + term(side_ref, 2)
        old = density_ref[...]
        out_ref[...] = old + damping * (driven_ref[...] - old - near)
        if last:
            count = chosen.shape[0]
            height = rows // count
            for m in range(count):
                at = pl.multiple_of(refs[5][m] * height, height)
                refs[6][:, m * height : (m + 1) * height] = out_ref[:, pl.ds(at, height)]

    last = chosen is not None
    whole = (width, rows)
    return pl.pallas_call(
        body,
        out_shape=jax.ShapeDtypeStruct(whole, jnp.float32),
        in_specs=[VMEM] * 5 + [SMEM] * last,
        out_specs=VMEM,
        scratch_shapes=[pltpu.VMEM(whole, jnp.float32)] * last,
        compiler_params=params(8 if rows <= 512 else 24),
        cost_estimate=cost(4 * width * rows * rows, 4 * rows * rows + 16 * width * rows),
        name="steady",
    )(dense, driven, density, rounded, near_side, *([chosen] if last else []))


def sweep(dense, base, far_side, pieces):
    width, rows = base.shape

    def body(dense_ref, base_ref, side_ref, *outs):
        near = lax.dot_general(
            side_ref[...], dense_ref[:, :rows], (((1,), (1,)), ((), ())), preferred_element_type=jnp.float32
        )
        new = base_ref[...] - damping * near
        if pieces:
            height = rows // pieces
            for m in range(pieces):
                outs[m][...] = new[:, m * height : (m + 1) * height]
        else:
            outs[0][...] = new
            outs[1][...] = new.astype(far_side.dtype)

    if pieces:
        out_shape = [jax.ShapeDtypeStruct((width, rows // pieces), jnp.float32)] * pieces
    else:
        out_shape = [jax.ShapeDtypeStruct((width, rows), kind) for kind in (jnp.float32, far_side.dtype)]
    return pl.pallas_call(
        body,
        out_shape=out_shape,
        in_specs=[VMEM] * 3,
        out_specs=[VMEM] * len(out_shape),
        compiler_params=params(8 if rows <= 512 else 24),
        cost_estimate=cost(2 * width * rows * rows, 2 * rows * rows + 12 * width * rows),
        name="sweep",
    )(dense, base, far_side)


def assemble(pieces):
    width, height = pieces[0].shape
    columns = width * len(pieces)

    def body(*refs):
        row = lax.axis_index("row")
        out_ref, turned = refs[-2:]
        for m in range(len(pieces)):
            at = pl.multiple_of((row ^ m) * width, width)
            turned[pl.ds(at, width), :] = refs[m][...]
        out_ref[0] = turned[...].T

    return pl.pallas_call(
        body,
        out_shape=jax.ShapeDtypeStruct((1, height, columns), jnp.float32),
        in_specs=[VMEM] * len(pieces),
        out_specs=VMEM,
        scratch_shapes=[pltpu.VMEM((columns, height), jnp.float32)],
        compiler_params=params(8),
        cost_estimate=cost(0, 8 * columns * height),
        name="assemble",
    )(*pieces)


def per_device(kernels, history, incident, owner, tile_pairs, tile_values, tile_counts):
    row_count = lax.axis_size("row")
    col_count = lax.axis_size("col")
    lags, _, _ = history.shape
    half = lags // PARTS

    def across_rows(x, m):
        return lax.ppermute(x, "row", [(i, i ^ m) for i in range(row_count)])

    walk = list(range(0, col_count, 2)) + list(range(col_count - 1, 0, -2))

    def swap_walk(x, side):
        return lax.ppermute(x, "col", [(walk[p], walk[mate(p, side, col_count)]) for p in range(col_count)])

    def swap_cols(x, side):
        return lax.ppermute(x, "col", [(c, mate(c, side, col_count)) for c in range(col_count)])

    chosen, own_tiles = prepare(owner, tile_pairs.T, tile_counts, tile_values)
    parts = [own_tiles]
    for m in range(1, row_count):
        parts.append(across_rows(own_tiles, m))
    dense, dense_last = stack_rows(chosen, parts)

    halves = [history[i * half : (i + 1) * half] for i in range(PARTS)]
    moving = {(side, i): halves[i] for i in range(PARTS) for side in (1, 2)}
    final = col_count // 2

    def turn(step, rank):
        out = {}
        for i in range(PARTS):
            side = early_side(step, i, final) if rank == 0 else 3 - early_side(step, i, final)
            out[side, i] = swap_walk(moving[3 - side, i], side)
        return out

    def over_rows(keep, give, kind):
        bit = 1
        odd = list(give)
        even = [keep[t] for t in range(row_count // 2)]
        while True:
            got = []
            for x in odd:
                got.append(across_rows(x, bit).astype(jnp.float32))
            summed = [x + y for x, y in zip(even, got)]
            if len(summed) == 1:
                return summed[0]
            bit *= 2
            even, odd = summed[0::2], [x.astype(kind) for x in summed[1::2]]

    total = multiply(kernels, [(0, 1, i, x) for i, x in enumerate(halves)], None, None, None, 0)
    for step in range(1, final):
        turns = [turn(step, rank) for rank in range(2)]
        moving = turns[0] | turns[1]
        for rank in range(2):
            blocks = [(step, side, i, x) for (side, i), x in turns[rank].items()]
            early = (step, rank) == (final - 1, 0)
            field = (incident[0], chosen) if early else (None, None)
            total = multiply(kernels, blocks, total, *field, row_count if early else 0)
            if early:
                early_sum = over_rows(total[0], total[1:], jnp.float32)
                total = None
    for i, ((_, part), x) in enumerate(reversed(turn(final, 0).items())):
        total = multiply(kernels, [(final, 1, part, x)], total, None, None, i * row_count)
    driven = -(over_rows(total[0], total[1:], jnp.bfloat16) + early_sum)

    density = driven
    rounded = density.astype(jnp.bfloat16)
    for step in range(SWEEPS):
        far_side, near_side = swap_cols(rounded, 2), swap_cols(rounded, 1)
        last = step == SWEEPS - 1
        base = steady(dense, driven, density, rounded, near_side, chosen if last else None)
        result = sweep(dense_last if last else dense, base, far_side, row_count if last else 0)
        if step < SWEEPS - 1:
            density, rounded = result

    pieces = [result[0]]
    for m in range(1, row_count):
        pieces.append(across_rows(result[m], m))
    return assemble(pieces)


def solution(mesh):
    in_specs = (
        P(None, "col", "row"),
        P(None, ("row", "col"), None),
        P(("row", "col"), None, None),
        P(),
        P(("row", "col"), None),
        P(("row", "col"), None, None),
        P(("row", "col")),
    )
    out_specs = P(("row", "col"), None, None)
    return jax.shard_map(
        per_device, mesh=mesh, in_specs=in_specs, out_specs=out_specs, check_vma=False
    )
```

```python
import jax
import jax.numpy as jnp
from jax import lax
from jax.experimental import pallas as pl
from jax.experimental.pallas import tpu as pltpu
from jax.sharding import PartitionSpec as P


SWEEPS = 3
PARTS = 2
LANES = 128


damping = 0.7


def cost(flops, moved):
    return pl.CostEstimate(flops=flops, bytes_accessed=moved, transcendentals=0)


def params(limit):
    return pltpu.CompilerParams(vmem_limit_bytes=limit * 2**20)


VMEM = pl.BlockSpec(memory_space=pltpu.VMEM)
SMEM = pl.BlockSpec(memory_space=pltpu.SMEM)


def mate(p, side, count):
    return p ^ 1 if side == 1 else (p + (1 if p % 2 else -1)) % count


def early_side(step, part, final):
    return 1 if (final - step + part) % 2 == 0 else 2


def prepare(owner, pairs, counts, tile_values):
    rows = lax.axis_size("row")
    cols = lax.axis_size("col")
    tiles, height, deep = tile_values.shape
    slots = 3 * rows

    def body(owner_ref, pairs_ref, counts_ref, tile_ref, chosen_ref, out_ref, pick, live):
        row, col = lax.axis_index("row"), lax.axis_index("col")
        for i in range(rows):
            chosen_ref[owner_ref[col * rows + i] ^ row] = i
        for q in range(slots):
            pick[q] = 0
            live[q] = 0
        ahead = jnp.where(lax.rem(col, 2) == 0, 1, cols - 1)
        for t in range(tiles):

            @pl.when(t < counts_ref[0])
            def _(t=t):
                source = pairs_ref[1, t]
                apart = lax.rem(source // rows - col + cols, cols)
                block = jnp.where(apart == 0, 1, jnp.where(apart == ahead, 2, 0))
                slot = block * rows + lax.rem(source, rows)
                pick[slot] = t
                live[slot] = 1

        for q in range(slots):
            tile = tile_ref[pick[q]]
            out_ref[:, q * deep : (q + 1) * deep] = jnp.where(live[q] > 0, tile, jnp.zeros_like(tile))

    return pl.pallas_call(
        body,
        out_shape=[
            jax.ShapeDtypeStruct((rows,), jnp.int32),
            jax.ShapeDtypeStruct((height, slots * deep), tile_values.dtype),
        ],
        in_specs=[SMEM] * 3 + [VMEM],
        out_specs=[SMEM, VMEM],
        scratch_shapes=[pltpu.SMEM((slots,), jnp.int32), pltpu.SMEM((slots,), jnp.int32)],
        compiler_params=params(4),
        cost_estimate=cost(0, 4 * slots * height * deep),
        name="prepare",
    )(owner, pairs, counts, tile_values)


def stack_rows(chosen, parts):
    count = len(parts)
    rows, width = parts[0].shape
    side = width // 3

    def body(chosen_ref, *refs):
        for m in range(count):
            at = pl.multiple_of(chosen_ref[m] * rows, rows)
            refs[-2][pl.ds(at, rows), :] = refs[m][...]
            refs[-1][m * rows : (m + 1) * rows, :] = refs[m][:, :side]

    return pl.pallas_call(
        body,
        out_shape=[
            jax.ShapeDtypeStruct((count * rows, width), parts[0].dtype),
            jax.ShapeDtypeStruct((count * rows, side), parts[0].dtype),
        ],
        in_specs=[SMEM] + [VMEM] * count,
        out_specs=[VMEM] * 2,
        compiler_params=params(4 if rows * count <= 512 else 24),
        cost_estimate=cost(0, 4 * count * rows * width),
        name="stack_rows",
    )(chosen, *parts)


def multiply(kernels, blocks, seed, incident, chosen, spread):
    rows = kernels.shape[1]
    cols = lax.axis_size("col")
    count = len(blocks)
    lags, depth, columns = blocks[0][3].shape
    tall = -(-(depth + LANES - 1) // LANES) * LANES
    extra = ([] if seed is None else [seed]) + ([] if incident is None else [incident, chosen])

    def body(kernel_ref, *refs):
        given, refs = refs[:count], refs[count:]
        seed_ref, refs = (None, refs) if seed is None else (refs[0], refs[1:])
        if incident is not None:
            (incident_ref, chosen_ref), refs = refs[:2], refs[2:]
        if spread:
            keep, give, (padded, total, turned) = refs[0], refs[1:-3], refs[-3:]
        else:
            total, padded = refs
        row, col = lax.axis_index("row"), lax.axis_index("col")
        stop = jnp.where(lax.rem(col, 2) == 0, col // 2, cols - 1 - col // 2)
        sign = jnp.where(lax.rem(stop, 2) == 1, 1, -1)
        padded[...] = jnp.zeros_like(padded)
        for s, (step, side, part, _) in enumerate(blocks):
            back = sign * (step if side == 1 else -step)
            at = lax.rem(stop - back + cols, cols)
            source = jnp.where(at < cols // 2, 2 * at, 2 * (cols - 1 - at) + 1)
            group = jnp.minimum(source * depth // LANES, (kernels.shape[2] - tall) // LANES)
            shift = source * depth - group * LANES
            for lag in range(lags):
                place = pl.multiple_of(lag * tall + shift, 32)
                padded[s, pl.ds(place, depth), :] = given[s][lag]
            lane = pl.multiple_of(group * LANES, LANES)
            left = jnp.concatenate([kernel_ref[part * lags + lag, :, pl.ds(lane, tall)] for lag in range(lags)], axis=1)
            product = jnp.dot(left, padded[s], preferred_element_type=jnp.float32)
            if s or seed is not None:
                product = (total if s else seed_ref)[...] + product
            total[...] = product
        if incident is not None:
            height = incident.shape[0]
            mine = pl.ds(pl.multiple_of(chosen_ref[0] * height, height), height)
            total[mine, :] = total[mine, :] - incident_ref[...]
        if spread:
            turned[...] = total[...].T
            width = columns // spread
            for m in range(spread):
                at = pl.multiple_of((row ^ m) * width, width)
                value = turned[pl.ds(at, width), :]
                if m % 2:
                    give[m // 2][...] = value
                else:
                    keep[m // 2] = value

    whole = (rows, columns)
    scratch = [pltpu.VMEM((count, lags * tall, columns), kernels.dtype)]
    if spread:
        piece = (columns // spread, rows)
        out_shape = [jax.ShapeDtypeStruct((spread // 2, *piece), jnp.float32)]
        out_shape += [jax.ShapeDtypeStruct(piece, jnp.float32)] * (spread // 2)
        scratch += [pltpu.VMEM(whole, jnp.float32), pltpu.VMEM(whole[::-1], jnp.float32)]
    else:
        out_shape = jax.ShapeDtypeStruct(whole, jnp.float32)
    in_specs = [VMEM] * (1 + count + len(extra))
    if incident is not None:
        in_specs[-1] = SMEM

    return pl.pallas_call(
        body,
        out_shape=out_shape,
        in_specs=in_specs,
        out_specs=[VMEM] * len(out_shape) if spread else VMEM,
        scratch_shapes=scratch,
        compiler_params=params(16 if rows <= 512 else 40),
        cost_estimate=cost(2 * count * lags * rows * tall * columns, 2 * count * lags * tall * (rows + columns)),
        name="multiply",
    )(kernels, *[block[3] for block in blocks], *extra)


def steady(dense, driven, density, rounded, near_side, chosen):
    width, rows = driven.shape

    def body(*refs):
        dense_ref, driven_ref, density_ref, rounded_ref, side_ref, out_ref = refs[:5] + refs[-1 if last else 5 :][:1]

        def term(ref, k):
            return lax.dot_general(
                ref[...],
                dense_ref[:, k * rows : (k + 1) * rows],
                (((1,), (1,)), ((), ())),
                preferred_element_type=jnp.float32,
            )

        near = term(rounded_ref, 1) + term(side_ref, 2)
        old = density_ref[...]
        out_ref[...] = old + damping * (driven_ref[...] - old - near)
        if last:
            count = chosen.shape[0]
            height = rows // count
            for m in range(count):
                at = pl.multiple_of(refs[5][m] * height, height)
                refs[6][:, m * height : (m + 1) * height] = out_ref[:, pl.ds(at, height)]

    last = chosen is not None
    whole = (width, rows)
    return pl.pallas_call(
        body,
        out_shape=jax.ShapeDtypeStruct(whole, jnp.float32),
        in_specs=[VMEM] * 5 + [SMEM] * last,
        out_specs=VMEM,
        scratch_shapes=[pltpu.VMEM(whole, jnp.float32)] * last,
        compiler_params=params(8 if rows <= 512 else 24),
        cost_estimate=cost(4 * width * rows * rows, 4 * rows * rows + 16 * width * rows),
        name="steady",
    )(dense, driven, density, rounded, near_side, *([chosen] if last else []))


def sweep(dense, base, far_side, pieces):
    width, rows = base.shape

    def body(dense_ref, base_ref, side_ref, *outs):
        near = lax.dot_general(
            side_ref[...], dense_ref[:, :rows], (((1,), (1,)), ((), ())), preferred_element_type=jnp.float32
        )
        new = base_ref[...] - damping * near
        if pieces:
            height = rows // pieces
            for m in range(pieces):
                outs[m][...] = new[:, m * height : (m + 1) * height]
        else:
            outs[0][...] = new
            outs[1][...] = new.astype(far_side.dtype)

    if pieces:
        out_shape = [jax.ShapeDtypeStruct((width, rows // pieces), jnp.float32)] * pieces
    else:
        out_shape = [jax.ShapeDtypeStruct((width, rows), kind) for kind in (jnp.float32, far_side.dtype)]
    return pl.pallas_call(
        body,
        out_shape=out_shape,
        in_specs=[VMEM] * 3,
        out_specs=[VMEM] * len(out_shape),
        compiler_params=params(8 if rows <= 512 else 24),
        cost_estimate=cost(2 * width * rows * rows, 2 * rows * rows + 12 * width * rows),
        name="sweep",
    )(dense, base, far_side)


def assemble(pieces):
    width, height = pieces[0].shape
    columns = width * len(pieces)

    def body(*refs):
        row = lax.axis_index("row")
        out_ref, turned = refs[-2:]
        for m in range(len(pieces)):
            at = pl.multiple_of((row ^ m) * width, width)
            turned[pl.ds(at, width), :] = refs[m][...]
        out_ref[0] = turned[...].T

    return pl.pallas_call(
        body,
        out_shape=jax.ShapeDtypeStruct((1, height, columns), jnp.float32),
        in_specs=[VMEM] * len(pieces),
        out_specs=VMEM,
        scratch_shapes=[pltpu.VMEM((columns, height), jnp.float32)],
        compiler_params=params(8),
        cost_estimate=cost(0, 8 * columns * height),
        name="assemble",
    )(*pieces)


def per_device(kernels, history, incident, owner, tile_pairs, tile_values, tile_counts):
    row_count = lax.axis_size("row")
    col_count = lax.axis_size("col")
    lags, _, _ = history.shape
    half = lags // PARTS

    def across_rows(x, m):
        return lax.ppermute(x, "row", [(i, i ^ m) for i in range(row_count)])

    walk = list(range(0, col_count, 2)) + list(range(col_count - 1, 0, -2))

    def swap_walk(x, side):
        return lax.ppermute(x, "col", [(walk[p], walk[mate(p, side, col_count)]) for p in range(col_count)])

    def swap_cols(x, side):
        return lax.ppermute(x, "col", [(c, mate(c, side, col_count)) for c in range(col_count)])

    chosen, own_tiles = prepare(owner, tile_pairs.T, tile_counts, tile_values)
    parts = [own_tiles]
    for m in range(1, row_count):
        parts.append(across_rows(own_tiles, m))
    dense, dense_last = stack_rows(chosen, parts)

    halves = [history[i * half : (i + 1) * half] for i in range(PARTS)]
    moving = {(side, i): halves[i] for i in range(PARTS) for side in (1, 2)}
    final = col_count // 2

    def turn(step, rank):
        out = {}
        for i in range(PARTS):
            side = early_side(step, i, final) if rank == 0 else 3 - early_side(step, i, final)
            out[side, i] = swap_walk(moving[3 - side, i], side)
        return out

    def over_rows(keep, give, kind):
        bit = 1
        odd = list(give)
        even = [keep[t] for t in range(row_count // 2)]
        lost = []
        while True:
            got = []
            for t, x in enumerate(odd):
                near = x
                if bit > 1 and kind != x.dtype:
                    near = lax.reduce_precision(x, jnp.finfo(kind).nexp, jnp.finfo(kind).nmant)
                    lost.append(((2 * t + 1) * bit, (x - near).astype(kind)))
                got.append(across_rows(near.astype(kind if bit > 1 else x.dtype), bit).astype(x.dtype))
            summed = [x + y for x, y in zip(even, got)]
            if len(summed) == 1:
                return summed[0], lost
            bit *= 2
            even, odd = summed[0::2], summed[1::2]

    total = multiply(kernels, [(0, 1, i, x) for i, x in enumerate(halves)], None, None, None, 0)
    for step in range(1, final):
        turns = [turn(step, rank) for rank in range(2)]
        moving = turns[0] | turns[1]
        for rank in range(2):
            blocks = [(step, side, i, x) for (side, i), x in turns[rank].items()]
            field = (incident[0], chosen) if (step, rank) == (final - 1, 0) else (None, None)
            total = multiply(kernels, blocks, total, *field, 0)
    for i, ((_, part), x) in enumerate(reversed(turn(final, 0).items())):
        total = multiply(kernels, [(final, 1, part, x)], total, None, None, i * row_count)
    summed, lost = over_rows(total[0], total[1:], jnp.bfloat16)
    driven = -summed

    density = driven
    rounded = density.astype(jnp.bfloat16)
    for step in range(SWEEPS):
        far_side, near_side = swap_cols(rounded, 2), swap_cols(rounded, 1)
        last = step == SWEEPS - 1
        if step == 0:
            rest = sum(across_rows(x, m).astype(jnp.float32) for m, x in lost)
        if step == 1:
            driven, density = driven - rest, density - rest
        base = steady(dense, driven, density, rounded, near_side, chosen if last else None)
        result = sweep(dense_last if last else dense, base, far_side, row_count if last else 0)
        if step < SWEEPS - 1:
            density, rounded = result

    pieces = [result[0]]
    for m in range(1, row_count):
        pieces.append(across_rows(result[m], m))
    return assemble(pieces)


def solution(mesh):
    in_specs = (
        P(None, "col", "row"),
        P(None, ("row", "col"), None),
        P(("row", "col"), None, None),
        P(),
        P(("row", "col"), None),
        P(("row", "col"), None, None),
        P(("row", "col")),
    )
    out_specs = P(("row", "col"), None, None)
    return jax.shard_map(
        per_device, mesh=mesh, in_specs=in_specs, out_specs=out_specs, check_vma=False
    )
```

```python
import math

import jax
import jax.numpy as jnp
from jax import lax
from jax.experimental import pallas as pl
from jax.experimental.pallas import tpu as pltpu
from jax.sharding import PartitionSpec as P


SWEEPS = 3
PARTS = 2
LANES = 128


damping = 0.7


def cost(flops, moved):
    return pl.CostEstimate(flops=flops, bytes_accessed=moved, transcendentals=0)


def params(limit):
    return pltpu.CompilerParams(vmem_limit_bytes=limit * 2**20)


VMEM = pl.BlockSpec(memory_space=pltpu.VMEM)
SMEM = pl.BlockSpec(memory_space=pltpu.SMEM)


def mate(p, side, count):
    return p ^ 1 if side == 1 else (p + (1 if p % 2 else -1)) % count


def early_side(step, part, final):
    return 1 if (final - step + part) % 2 == 0 else 2


def prepare(owner, pairs, counts, tile_values):
    rows = lax.axis_size("row")
    cols = lax.axis_size("col")
    tiles, height, deep = tile_values.shape
    slots = 3 * rows

    def body(owner_ref, pairs_ref, counts_ref, tile_ref, chosen_ref, out_ref, pick, live):
        row, col = lax.axis_index("row"), lax.axis_index("col")
        for i in range(rows):
            chosen_ref[owner_ref[col * rows + i] ^ row] = i
        for q in range(slots):
            pick[q] = 0
            live[q] = 0
        ahead = jnp.where(lax.rem(col, 2) == 0, 1, cols - 1)
        for t in range(tiles):

            @pl.when(t < counts_ref[0])
            def _(t=t):
                source = pairs_ref[1, t]
                apart = lax.rem(source // rows - col + cols, cols)
                block = jnp.where(apart == 0, 1, jnp.where(apart == ahead, 2, 0))
                slot = block * rows + lax.rem(source, rows)
                pick[slot] = t
                live[slot] = 1

        for q in range(slots):
            tile = tile_ref[pick[q]]
            out_ref[:, q * deep : (q + 1) * deep] = jnp.where(live[q] > 0, tile, jnp.zeros_like(tile))

    return pl.pallas_call(
        body,
        out_shape=[
            jax.ShapeDtypeStruct((rows,), jnp.int32),
            jax.ShapeDtypeStruct((height, slots * deep), tile_values.dtype),
        ],
        in_specs=[SMEM] * 3 + [VMEM],
        out_specs=[SMEM, VMEM],
        scratch_shapes=[pltpu.SMEM((slots,), jnp.int32), pltpu.SMEM((slots,), jnp.int32)],
        compiler_params=params(4),
        cost_estimate=cost(0, 4 * slots * height * deep),
        name="prepare",
    )(owner, pairs, counts, tile_values)


def stack_rows(chosen, parts):
    count = len(parts)
    rows, width = parts[0].shape
    side = width // 3

    def body(chosen_ref, *refs):
        for m in range(count):
            at = pl.multiple_of(chosen_ref[m] * rows, rows)
            refs[-2][pl.ds(at, rows), :] = refs[m][...]
            refs[-1][m * rows : (m + 1) * rows, :] = refs[m][:, :side]

    return pl.pallas_call(
        body,
        out_shape=[
            jax.ShapeDtypeStruct((count * rows, width), parts[0].dtype),
            jax.ShapeDtypeStruct((count * rows, side), parts[0].dtype),
        ],
        in_specs=[SMEM] + [VMEM] * count,
        out_specs=[VMEM] * 2,
        compiler_params=params(4 if rows * count <= 512 else 24),
        cost_estimate=cost(0, 4 * count * rows * width),
        name="stack_rows",
    )(chosen, *parts)


def multiply(kernels, blocks, seed, incident, chosen, spread):
    rows = kernels.shape[1]
    cols = lax.axis_size("col")
    count = len(blocks)
    lags, depth, columns = blocks[0][3].shape
    tall = -(-(depth + LANES - math.gcd(depth, LANES)) // LANES) * LANES
    extra = ([] if seed is None else [seed]) + ([] if incident is None else [incident, chosen])

    def body(kernel_ref, *refs):
        given, refs = refs[:count], refs[count:]
        seed_ref, refs = (None, refs) if seed is None else (refs[0], refs[1:])
        if incident is not None:
            (incident_ref, chosen_ref), refs = refs[:2], refs[2:]
        if spread:
            keep, give, (padded, total, turned) = refs[0], refs[1:-3], refs[-3:]
        else:
            total, padded = refs
        row, col = lax.axis_index("row"), lax.axis_index("col")
        stop = jnp.where(lax.rem(col, 2) == 0, col // 2, cols - 1 - col // 2)
        sign = jnp.where(lax.rem(stop, 2) == 1, 1, -1)
        padded[...] = jnp.zeros_like(padded)
        for s, (step, side, part, _) in enumerate(blocks):
            back = sign * (step if side == 1 else -step)
            at = lax.rem(stop - back + cols, cols)
            source = jnp.where(at < cols // 2, 2 * at, 2 * (cols - 1 - at) + 1)
            group = jnp.minimum(source * depth // LANES, (kernels.shape[2] - tall) // LANES)
            shift = source * depth - group * LANES
            for lag in range(lags):
                place = pl.multiple_of(lag * tall + shift, 32)
                padded[s, pl.ds(place, depth), :] = given[s][lag]
            lane = pl.multiple_of(group * LANES, LANES)
            left = jnp.concatenate([kernel_ref[part * lags + lag, :, pl.ds(lane, tall)] for lag in range(lags)], axis=1)
            product = jnp.dot(left, padded[s], preferred_element_type=jnp.float32)
            if s or seed is not None:
                product = (total if s else seed_ref)[...] + product
            total[...] = product
        if incident is not None:
            height = incident.shape[0]
            mine = pl.ds(pl.multiple_of(chosen_ref[0] * height, height), height)
            total[mine, :] = total[mine, :] - incident_ref[...]
        if spread:
            turned[...] = total[...].T
            width = columns // spread
            for m in range(spread):
                at = pl.multiple_of((row ^ m) * width, width)
                value = turned[pl.ds(at, width), :]
                if m % 2:
                    give[m // 2][...] = value
                else:
                    keep[m // 2] = value

    whole = (rows, columns)
    scratch = [pltpu.VMEM((count, lags * tall, columns), kernels.dtype)]
    if spread:
        piece = (columns // spread, rows)
        out_shape = [jax.ShapeDtypeStruct((spread // 2, *piece), jnp.float32)]
        out_shape += [jax.ShapeDtypeStruct(piece, jnp.float32)] * (spread // 2)
        scratch += [pltpu.VMEM(whole, jnp.float32), pltpu.VMEM(whole[::-1], jnp.float32)]
    else:
        out_shape = jax.ShapeDtypeStruct(whole, jnp.float32)
    in_specs = [VMEM] * (1 + count + len(extra))
    if incident is not None:
        in_specs[-1] = SMEM

    return pl.pallas_call(
        body,
        out_shape=out_shape,
        in_specs=in_specs,
        out_specs=[VMEM] * len(out_shape) if spread else VMEM,
        scratch_shapes=scratch,
        compiler_params=params(16 if rows <= 512 else 40),
        cost_estimate=cost(2 * count * lags * rows * tall * columns, 2 * count * lags * tall * (rows + columns)),
        name="multiply",
    )(kernels, *[block[3] for block in blocks], *extra)


def steady(dense, driven, density, rounded, near_side, chosen):
    width, rows = driven.shape

    def body(*refs):
        dense_ref, driven_ref, density_ref, rounded_ref, side_ref, out_ref = refs[:5] + refs[-1 if last else 5 :][:1]

        def term(ref, k):
            return lax.dot_general(
                ref[...],
                dense_ref[:, k * rows : (k + 1) * rows],
                (((1,), (1,)), ((), ())),
                preferred_element_type=jnp.float32,
            )

        near = term(rounded_ref, 1) + term(side_ref, 2)
        old = density_ref[...]
        out_ref[...] = old + damping * (driven_ref[...] - old - near)
        if last:
            count = chosen.shape[0]
            height = rows // count
            for m in range(count):
                at = pl.multiple_of(refs[5][m] * height, height)
                refs[6][:, m * height : (m + 1) * height] = out_ref[:, pl.ds(at, height)]

    last = chosen is not None
    whole = (width, rows)
    return pl.pallas_call(
        body,
        out_shape=jax.ShapeDtypeStruct(whole, jnp.float32),
        in_specs=[VMEM] * 5 + [SMEM] * last,
        out_specs=VMEM,
        scratch_shapes=[pltpu.VMEM(whole, jnp.float32)] * last,
        compiler_params=params(8 if rows <= 512 else 24),
        cost_estimate=cost(4 * width * rows * rows, 4 * rows * rows + 16 * width * rows),
        name="steady",
    )(dense, driven, density, rounded, near_side, *([chosen] if last else []))


def sweep(dense, base, far_side, pieces):
    width, rows = base.shape

    def body(dense_ref, base_ref, side_ref, *outs):
        near = lax.dot_general(
            side_ref[...], dense_ref[:, :rows], (((1,), (1,)), ((), ())), preferred_element_type=jnp.float32
        )
        new = base_ref[...] - damping * near
        if pieces:
            height = rows // pieces
            for m in range(pieces):
                outs[m][...] = new[:, m * height : (m + 1) * height]
        else:
            outs[0][...] = new
            outs[1][...] = new.astype(far_side.dtype)

    if pieces:
        out_shape = [jax.ShapeDtypeStruct((width, rows // pieces), jnp.float32)] * pieces
    else:
        out_shape = [jax.ShapeDtypeStruct((width, rows), kind) for kind in (jnp.float32, far_side.dtype)]
    return pl.pallas_call(
        body,
        out_shape=out_shape,
        in_specs=[VMEM] * 3,
        out_specs=[VMEM] * len(out_shape),
        compiler_params=params(8 if rows <= 512 else 24),
        cost_estimate=cost(2 * width * rows * rows, 2 * rows * rows + 12 * width * rows),
        name="sweep",
    )(dense, base, far_side)


def assemble(pieces):
    width, height = pieces[0].shape
    columns = width * len(pieces)

    def body(*refs):
        row = lax.axis_index("row")
        out_ref, turned = refs[-2:]
        for m in range(len(pieces)):
            at = pl.multiple_of((row ^ m) * width, width)
            turned[pl.ds(at, width), :] = refs[m][...]
        out_ref[0] = turned[...].T

    return pl.pallas_call(
        body,
        out_shape=jax.ShapeDtypeStruct((1, height, columns), jnp.float32),
        in_specs=[VMEM] * len(pieces),
        out_specs=VMEM,
        scratch_shapes=[pltpu.VMEM((columns, height), jnp.float32)],
        compiler_params=params(8),
        cost_estimate=cost(0, 8 * columns * height),
        name="assemble",
    )(*pieces)


def per_device(kernels, history, incident, owner, tile_pairs, tile_values, tile_counts):
    row_count = lax.axis_size("row")
    col_count = lax.axis_size("col")
    lags, _, _ = history.shape
    half = lags // PARTS

    def across_rows(x, m):
        return lax.ppermute(x, "row", [(i, i ^ m) for i in range(row_count)])

    walk = list(range(0, col_count, 2)) + list(range(col_count - 1, 0, -2))

    def swap_walk(x, side):
        return lax.ppermute(x, "col", [(walk[p], walk[mate(p, side, col_count)]) for p in range(col_count)])

    def swap_cols(x, side):
        return lax.ppermute(x, "col", [(c, mate(c, side, col_count)) for c in range(col_count)])

    chosen, own_tiles = prepare(owner, tile_pairs.T, tile_counts, tile_values)
    parts = [own_tiles]
    for m in range(1, row_count):
        parts.append(across_rows(own_tiles, m))
    dense, dense_last = stack_rows(chosen, parts)

    halves = [history[i * half : (i + 1) * half] for i in range(PARTS)]
    moving = {(side, i): halves[i] for i in range(PARTS) for side in (1, 2)}
    final = col_count // 2

    def turn(step, rank):
        out = {}
        for i in range(PARTS):
            side = early_side(step, i, final) if rank == 0 else 3 - early_side(step, i, final)
            out[side, i] = swap_walk(moving[3 - side, i], side)
        return out

    def over_rows(keep, give, kind):
        bit = 1
        odd = list(give)
        even = [keep[t] for t in range(row_count // 2)]
        lost = []
        while True:
            got = []
            for t, x in enumerate(odd):
                near = x
                if bit > 1 and kind != x.dtype:
                    near = lax.reduce_precision(x, jnp.finfo(kind).nexp, jnp.finfo(kind).nmant)
                    lost.append(((2 * t + 1) * bit, (x - near).astype(kind)))
                got.append(across_rows(near.astype(kind if bit > 1 else x.dtype), bit).astype(x.dtype))
            summed = [x + y for x, y in zip(even, got)]
            if len(summed) == 1:
                return summed[0], lost
            bit *= 2
            even, odd = summed[0::2], summed[1::2]

    total = multiply(kernels, [(0, 1, i, x) for i, x in enumerate(halves)], None, None, None, 0)
    for step in range(1, final):
        turns = [turn(step, rank) for rank in range(2)]
        moving = turns[0] | turns[1]
        for rank in range(2):
            blocks = [(step, side, i, x) for (side, i), x in turns[rank].items()]
            early = (step, rank) == (final - 1, 0)
            field = (incident[0], chosen) if early else (None, None)
            total = multiply(kernels, blocks, total, *field, row_count if early else 0)
            if early:
                early_sum, _ = over_rows(total[0], total[1:], jnp.float32)
                total = None
    for i, ((_, part), x) in enumerate(reversed(turn(final, 0).items())):
        total = multiply(kernels, [(final, 1, part, x)], total, None, None, i * row_count)
    late_sum, lost = over_rows(total[0], total[1:], jnp.bfloat16)
    driven = -(late_sum + early_sum)

    density = driven
    rounded = density.astype(jnp.bfloat16)
    for step in range(SWEEPS):
        far_side, near_side = swap_cols(rounded, 2), swap_cols(rounded, 1)
        last = step == SWEEPS - 1
        if step == 0:
            rest = sum(across_rows(x, m).astype(jnp.float32) for m, x in lost)
        if step == 1:
            driven, density = driven - rest, density - rest
        base = steady(dense, driven, density, rounded, near_side, chosen if last else None)
        result = sweep(dense_last if last else dense, base, far_side, row_count if last else 0)
        if step < SWEEPS - 1:
            density, rounded = result

    pieces = [result[0]]
    for m in range(1, row_count):
        pieces.append(across_rows(result[m], m))
    return assemble(pieces)


def solution(mesh):
    in_specs = (
        P(None, "col", "row"),
        P(None, ("row", "col"), None),
        P(("row", "col"), None, None),
        P(),
        P(("row", "col"), None),
        P(("row", "col"), None, None),
        P(("row", "col")),
    )
    out_specs = P(("row", "col"), None, None)
    return jax.shard_map(
        per_device, mesh=mesh, in_specs=in_specs, out_specs=out_specs, check_vma=False
    )
```

```python
import math

import jax
import jax.numpy as jnp
from jax import lax
from jax.experimental import pallas as pl
from jax.experimental.pallas import tpu as pltpu
from jax.sharding import PartitionSpec as P


SWEEPS = 3
PARTS = 2
LANES = 128


damping = 0.7


def cost(flops, moved):
    return pl.CostEstimate(flops=flops, bytes_accessed=moved, transcendentals=0)


def params(limit):
    return pltpu.CompilerParams(vmem_limit_bytes=limit * 2**20)


VMEM = pl.BlockSpec(memory_space=pltpu.VMEM)
SMEM = pl.BlockSpec(memory_space=pltpu.SMEM)


def mate(p, side, count):
    return p ^ 1 if side == 1 else (p + (1 if p % 2 else -1)) % count


def early_side(step, part, final):
    return 1 if (final - step + part) % 2 == 0 else 2


def prepare(owner, pairs, counts, tile_values):
    rows = lax.axis_size("row")
    cols = lax.axis_size("col")
    tiles, height, deep = tile_values.shape
    slots = 3 * rows

    def body(owner_ref, pairs_ref, counts_ref, tile_ref, chosen_ref, out_ref, pick, live):
        row, col = lax.axis_index("row"), lax.axis_index("col")
        for i in range(rows):
            chosen_ref[owner_ref[col * rows + i] ^ row] = i
        for q in range(slots):
            pick[q] = 0
            live[q] = 0
        ahead = jnp.where(lax.rem(col, 2) == 0, 1, cols - 1)
        for t in range(tiles):

            @pl.when(t < counts_ref[0])
            def _(t=t):
                source = pairs_ref[1, t]
                apart = lax.rem(source // rows - col + cols, cols)
                block = jnp.where(apart == 0, 1, jnp.where(apart == ahead, 2, 0))
                slot = block * rows + lax.rem(source, rows)
                pick[slot] = t
                live[slot] = 1

        for q in range(slots):
            tile = tile_ref[pick[q]]
            out_ref[:, q * deep : (q + 1) * deep] = jnp.where(live[q] > 0, tile, jnp.zeros_like(tile))

    return pl.pallas_call(
        body,
        out_shape=[
            jax.ShapeDtypeStruct((rows,), jnp.int32),
            jax.ShapeDtypeStruct((height, slots * deep), tile_values.dtype),
        ],
        in_specs=[SMEM] * 3 + [VMEM],
        out_specs=[SMEM, VMEM],
        scratch_shapes=[pltpu.SMEM((slots,), jnp.int32), pltpu.SMEM((slots,), jnp.int32)],
        compiler_params=params(4),
        cost_estimate=cost(0, 4 * slots * height * deep),
        name="prepare",
    )(owner, pairs, counts, tile_values)


def stack_rows(chosen, parts):
    count = len(parts)
    rows, width = parts[0].shape
    side = width // 3

    def body(chosen_ref, *refs):
        for m in range(count):
            at = pl.multiple_of(chosen_ref[m] * rows, rows)
            refs[-2][pl.ds(at, rows), :] = refs[m][...]
            refs[-1][m * rows : (m + 1) * rows, :] = refs[m][:, :side]

    return pl.pallas_call(
        body,
        out_shape=[
            jax.ShapeDtypeStruct((count * rows, width), parts[0].dtype),
            jax.ShapeDtypeStruct((count * rows, side), parts[0].dtype),
        ],
        in_specs=[SMEM] + [VMEM] * count,
        out_specs=[VMEM] * 2,
        compiler_params=params(4 if rows * count <= 512 else 24),
        cost_estimate=cost(0, 4 * count * rows * width),
        name="stack_rows",
    )(chosen, *parts)


def multiply(kernels, blocks, seed, incident, chosen, spread):
    rows = kernels.shape[1]
    cols = lax.axis_size("col")
    count = len(blocks)
    lags, depth, columns = blocks[0][3].shape
    tall = -(-(depth + LANES - math.gcd(depth, LANES)) // LANES) * LANES
    extra = ([] if seed is None else [seed]) + ([] if incident is None else [incident, chosen])

    def body(kernel_ref, *refs):
        given, refs = refs[:count], refs[count:]
        seed_ref, refs = (None, refs) if seed is None else (refs[0], refs[1:])
        if incident is not None:
            (incident_ref, chosen_ref), refs = refs[:2], refs[2:]
        if spread:
            keep, give, (padded, total, turned) = refs[0], refs[1:-3], refs[-3:]
        else:
            total, padded = refs
        row, col = lax.axis_index("row"), lax.axis_index("col")
        stop = jnp.where(lax.rem(col, 2) == 0, col // 2, cols - 1 - col // 2)
        sign = jnp.where(lax.rem(stop, 2) == 1, 1, -1)
        padded[...] = jnp.zeros_like(padded)
        for s, (step, side, part, _) in enumerate(blocks):
            back = sign * (step if side == 1 else -step)
            at = lax.rem(stop - back + cols, cols)
            source = jnp.where(at < cols // 2, 2 * at, 2 * (cols - 1 - at) + 1)
            group = jnp.minimum(source * depth // LANES, (kernels.shape[2] - tall) // LANES)
            shift = source * depth - group * LANES
            for lag in range(lags):
                place = pl.multiple_of(lag * tall + shift, 32)
                padded[s, pl.ds(place, depth), :] = given[s][lag]
            lane = pl.multiple_of(group * LANES, LANES)
            left = jnp.concatenate([kernel_ref[part * lags + lag, :, pl.ds(lane, tall)] for lag in range(lags)], axis=1)
            product = jnp.dot(left, padded[s], preferred_element_type=jnp.float32)
            if s or seed is not None:
                product = (total if s else seed_ref)[...] + product
            total[...] = product
        if incident is not None:
            height = incident.shape[0]
            mine = pl.ds(pl.multiple_of(chosen_ref[0] * height, height), height)
            total[mine, :] = total[mine, :] - incident_ref[...]
        if spread:
            turned[...] = total[...].T
            width = columns // spread
            for m in range(spread):
                at = pl.multiple_of((row ^ m) * width, width)
                value = turned[pl.ds(at, width), :]
                if m % 2:
                    give[m // 2][...] = value
                else:
                    keep[m // 2] = value

    whole = (rows, columns)
    scratch = [pltpu.VMEM((count, lags * tall, columns), kernels.dtype)]
    if spread:
        piece = (columns // spread, rows)
        out_shape = [jax.ShapeDtypeStruct((spread // 2, *piece), jnp.float32)]
        out_shape += [jax.ShapeDtypeStruct(piece, jnp.float32)] * (spread // 2)
        scratch += [pltpu.VMEM(whole, jnp.float32), pltpu.VMEM(whole[::-1], jnp.float32)]
    else:
        out_shape = jax.ShapeDtypeStruct(whole, jnp.float32)
    in_specs = [VMEM] * (1 + count + len(extra))
    if incident is not None:
        in_specs[-1] = SMEM

    return pl.pallas_call(
        body,
        out_shape=out_shape,
        in_specs=in_specs,
        out_specs=[VMEM] * len(out_shape) if spread else VMEM,
        scratch_shapes=scratch,
        compiler_params=params(16 if rows <= 512 else 40),
        cost_estimate=cost(2 * count * lags * rows * tall * columns, 2 * count * lags * tall * (rows + columns)),
        name="multiply",
    )(kernels, *[block[3] for block in blocks], *extra)


def steady(dense, driven, density, rounded, near_side, chosen):
    width, rows = driven.shape

    def body(*refs):
        dense_ref, driven_ref, density_ref, rounded_ref, side_ref, out_ref = refs[:5] + refs[-1 if last else 5 :][:1]

        def term(ref, k):
            return lax.dot_general(
                ref[...],
                dense_ref[:, k * rows : (k + 1) * rows],
                (((1,), (1,)), ((), ())),
                preferred_element_type=jnp.float32,
            )

        near = term(rounded_ref, 1) + term(side_ref, 2)
        old = density_ref[...]
        out_ref[...] = old + damping * (driven_ref[...] - old - near)
        if last:
            count = chosen.shape[0]
            height = rows // count
            for m in range(count):
                at = pl.multiple_of(refs[5][m] * height, height)
                refs[6][:, m * height : (m + 1) * height] = out_ref[:, pl.ds(at, height)]

    last = chosen is not None
    whole = (width, rows)
    return pl.pallas_call(
        body,
        out_shape=jax.ShapeDtypeStruct(whole, jnp.float32),
        in_specs=[VMEM] * 5 + [SMEM] * last,
        out_specs=VMEM,
        scratch_shapes=[pltpu.VMEM(whole, jnp.float32)] * last,
        compiler_params=params(8 if rows <= 512 else 24),
        cost_estimate=cost(4 * width * rows * rows, 4 * rows * rows + 16 * width * rows),
        name="steady",
    )(dense, driven, density, rounded, near_side, *([chosen] if last else []))


def sweep(dense, base, far_side, pieces):
    width, rows = base.shape

    def body(dense_ref, base_ref, side_ref, *outs):
        near = lax.dot_general(
            side_ref[...], dense_ref[:, :rows], (((1,), (1,)), ((), ())), preferred_element_type=jnp.float32
        )
        new = base_ref[...] - damping * near
        if pieces:
            height = rows // pieces
            for m in range(pieces):
                outs[m][...] = new[:, m * height : (m + 1) * height]
        else:
            outs[0][...] = new
            outs[1][...] = new.astype(far_side.dtype)

    if pieces:
        out_shape = [jax.ShapeDtypeStruct((width, rows // pieces), jnp.float32)] * pieces
    else:
        out_shape = [jax.ShapeDtypeStruct((width, rows), kind) for kind in (jnp.float32, far_side.dtype)]
    return pl.pallas_call(
        body,
        out_shape=out_shape,
        in_specs=[VMEM] * 3,
        out_specs=[VMEM] * len(out_shape),
        compiler_params=params(8 if rows <= 512 else 24),
        cost_estimate=cost(2 * width * rows * rows, 2 * rows * rows + 12 * width * rows),
        name="sweep",
    )(dense, base, far_side)


def assemble(pieces):
    width, height = pieces[0].shape
    columns = width * len(pieces)

    def body(*refs):
        row = lax.axis_index("row")
        out_ref, turned = refs[-2:]
        for m in range(len(pieces)):
            at = pl.multiple_of((row ^ m) * width, width)
            turned[pl.ds(at, width), :] = refs[m][...]
        out_ref[0] = turned[...].T

    return pl.pallas_call(
        body,
        out_shape=jax.ShapeDtypeStruct((1, height, columns), jnp.float32),
        in_specs=[VMEM] * len(pieces),
        out_specs=VMEM,
        scratch_shapes=[pltpu.VMEM((columns, height), jnp.float32)],
        compiler_params=params(8),
        cost_estimate=cost(0, 8 * columns * height),
        name="assemble",
    )(*pieces)


def per_device(kernels, history, incident, owner, tile_pairs, tile_values, tile_counts):
    row_count = lax.axis_size("row")
    col_count = lax.axis_size("col")
    lags, _, _ = history.shape
    half = lags // PARTS

    def across_rows(x, m):
        return lax.ppermute(x, "row", [(i, i ^ m) for i in range(row_count)])

    walk = list(range(0, col_count, 2)) + list(range(col_count - 1, 0, -2))

    def swap_walk(x, side):
        return lax.ppermute(x, "col", [(walk[p], walk[mate(p, side, col_count)]) for p in range(col_count)])

    def swap_cols(x, side):
        return lax.ppermute(x, "col", [(c, mate(c, side, col_count)) for c in range(col_count)])

    chosen, own_tiles = prepare(owner, tile_pairs.T, tile_counts, tile_values)
    parts = [own_tiles]
    for m in range(1, row_count):
        parts.append(across_rows(own_tiles, m))
    dense, dense_last = stack_rows(chosen, parts)

    halves = [history[i * half : (i + 1) * half] for i in range(PARTS)]
    moving = {(side, i): halves[i] for i in range(PARTS) for side in (1, 2)}
    final = col_count // 2

    def turn(step, rank):
        out = {}
        for i in range(PARTS):
            side = early_side(step, i, final) if rank == 0 else 3 - early_side(step, i, final)
            out[side, i] = swap_walk(moving[3 - side, i], side)
        return out

    def over_rows(keep, give, kind):
        bit = 1
        odd = list(give)
        even = [keep[t] for t in range(row_count // 2)]
        lost = []
        while True:
            got = []
            for t, x in enumerate(odd):
                near = x
                if bit > 1 and kind != x.dtype:
                    near = lax.reduce_precision(x, jnp.finfo(kind).nexp, jnp.finfo(kind).nmant)
                    lost.append(((2 * t + 1) * bit, (x - near).astype(kind)))
                got.append(across_rows(near.astype(kind if bit > 1 else x.dtype), bit).astype(x.dtype))
            summed = [x + y for x, y in zip(even, got)]
            if len(summed) == 1:
                return summed[0], lost
            bit *= 2
            even, odd = summed[0::2], summed[1::2]

    total = multiply(kernels, [(0, 1, i, x) for i, x in enumerate(halves)], None, None, None, 0)
    for step in range(1, final):
        turns = [turn(step, rank) for rank in range(2)]
        moving = turns[0] | turns[1]
        for rank in range(2):
            blocks = [(step, side, i, x) for (side, i), x in turns[rank].items()]
            early = (step, rank) == (final - 1, 1)
            field = (incident[0], chosen) if early else (None, None)
            total = multiply(kernels, blocks, total, *field, row_count if early else 0)
            if early:
                early_sum, _ = over_rows(total[0], total[1:], jnp.float32)
                total = None
    for i, ((_, part), x) in enumerate(reversed(turn(final, 0).items())):
        total = multiply(kernels, [(final, 1, part, x)], total, None, None, i * row_count)
    late_sum, lost = over_rows(total[0], total[1:], jnp.bfloat16)
    driven = -(late_sum + early_sum)

    density = driven
    rounded = density.astype(jnp.bfloat16)
    for step in range(SWEEPS):
        far_side = swap_cols(rounded, 2)
        near_side = swap_cols(rounded, 1)
        last = step == SWEEPS - 1
        if step == 0:
            rest = sum(across_rows(x, m).astype(jnp.float32) for m, x in lost)
        if step == 1:
            driven, density = driven - rest, density - rest
        base = steady(dense, driven, density, rounded, near_side, chosen if last else None)
        result = sweep(dense_last if last else dense, base, far_side, row_count if last else 0)
        if step < SWEEPS - 1:
            density, rounded = result

    pieces = [result[0]]
    for m in range(1, row_count):
        pieces.append(across_rows(result[m], m))
    return assemble(pieces)


def solution(mesh):
    in_specs = (
        P(None, "col", "row"),
        P(None, ("row", "col"), None),
        P(("row", "col"), None, None),
        P(),
        P(("row", "col"), None),
        P(("row", "col"), None, None),
        P(("row", "col")),
    )
    out_specs = P(("row", "col"), None, None)
    return jax.shard_map(
        per_device, mesh=mesh, in_specs=in_specs, out_specs=out_specs, check_vma=False
    )
```

```python
import math

import jax
import jax.numpy as jnp
from jax import lax
from jax.experimental import pallas as pl
from jax.experimental.pallas import tpu as pltpu
from jax.sharding import PartitionSpec as P


SWEEPS = 3
PARTS = 2
LANES = 128


damping = 0.7


def cost(flops, moved):
    return pl.CostEstimate(flops=flops, bytes_accessed=moved, transcendentals=0)


def params(limit):
    return pltpu.CompilerParams(vmem_limit_bytes=limit * 2**20)


VMEM = pl.BlockSpec(memory_space=pltpu.VMEM)
SMEM = pl.BlockSpec(memory_space=pltpu.SMEM)


def mate(p, side, count):
    return p ^ 1 if side == 1 else (p + (1 if p % 2 else -1)) % count


def early_side(step, part, final):
    return 1 if (final - step + part) % 2 == 0 else 2


def prepare(owner, pairs, counts, tile_values):
    rows = lax.axis_size("row")
    cols = lax.axis_size("col")
    tiles, height, deep = tile_values.shape
    slots = 3 * rows

    def body(owner_ref, pairs_ref, counts_ref, tile_ref, chosen_ref, out_ref, pick, live):
        row, col = lax.axis_index("row"), lax.axis_index("col")
        for i in range(rows):
            chosen_ref[owner_ref[col * rows + i] ^ row] = i
        for q in range(slots):
            pick[q] = 0
            live[q] = 0
        ahead = jnp.where(lax.rem(col, 2) == 0, 1, cols - 1)
        for t in range(tiles):

            @pl.when(t < counts_ref[0])
            def _(t=t):
                source = pairs_ref[1, t]
                apart = lax.rem(source // rows - col + cols, cols)
                block = jnp.where(apart == 0, 1, jnp.where(apart == ahead, 2, 0))
                slot = block * rows + lax.rem(source, rows)
                pick[slot] = t
                live[slot] = 1

        for q in range(slots):
            tile = tile_ref[pick[q]]
            out_ref[:, q * deep : (q + 1) * deep] = jnp.where(live[q] > 0, tile, jnp.zeros_like(tile))

    return pl.pallas_call(
        body,
        out_shape=[
            jax.ShapeDtypeStruct((rows,), jnp.int32),
            jax.ShapeDtypeStruct((height, slots * deep), tile_values.dtype),
        ],
        in_specs=[SMEM] * 3 + [VMEM],
        out_specs=[SMEM, VMEM],
        scratch_shapes=[pltpu.SMEM((slots,), jnp.int32), pltpu.SMEM((slots,), jnp.int32)],
        compiler_params=params(4),
        cost_estimate=cost(0, 4 * slots * height * deep),
        name="prepare",
    )(owner, pairs, counts, tile_values)


def stack_rows(chosen, parts):
    count = len(parts)
    rows, width = parts[0].shape
    side = width // 3

    def body(chosen_ref, *refs):
        for m in range(count):
            at = pl.multiple_of(chosen_ref[m] * rows, rows)
            refs[-2][pl.ds(at, rows), :] = refs[m][...]
            refs[-1][m * rows : (m + 1) * rows, :] = refs[m][:, :side]

    return pl.pallas_call(
        body,
        out_shape=[
            jax.ShapeDtypeStruct((count * rows, width), parts[0].dtype),
            jax.ShapeDtypeStruct((count * rows, side), parts[0].dtype),
        ],
        in_specs=[SMEM] + [VMEM] * count,
        out_specs=[VMEM] * 2,
        compiler_params=params(4 if rows * count <= 512 else 24),
        cost_estimate=cost(0, 4 * count * rows * width),
        name="stack_rows",
    )(chosen, *parts)


def multiply(kernels, blocks, seed, incident, chosen, spread):
    rows = kernels.shape[1]
    cols = lax.axis_size("col")
    count = len(blocks)
    lags, depth, columns = blocks[0][3].shape
    tall = -(-(depth + LANES - math.gcd(depth, LANES)) // LANES) * LANES
    extra = ([] if seed is None else [seed]) + ([] if incident is None else [incident, chosen])

    def body(kernel_ref, *refs):
        given, refs = refs[:count], refs[count:]
        seed_ref, refs = (None, refs) if seed is None else (refs[0], refs[1:])
        if incident is not None:
            (incident_ref, chosen_ref), refs = refs[:2], refs[2:]
        if spread:
            keep, give, (padded, total, turned) = refs[0], refs[1:-3], refs[-3:]
        else:
            total, padded = refs
        row, col = lax.axis_index("row"), lax.axis_index("col")
        stop = jnp.where(lax.rem(col, 2) == 0, col // 2, cols - 1 - col // 2)
        sign = jnp.where(lax.rem(stop, 2) == 1, 1, -1)
        padded[...] = jnp.zeros_like(padded)
        for s, (step, side, part, _) in enumerate(blocks):
            back = sign * (step if side == 1 else -step)
            at = lax.rem(stop - back + cols, cols)
            source = jnp.where(at < cols // 2, 2 * at, 2 * (cols - 1 - at) + 1)
            group = jnp.minimum(source * depth // LANES, (kernels.shape[2] - tall) // LANES)
            shift = source * depth - group * LANES
            for lag in range(lags):
                place = pl.multiple_of(lag * tall + shift, 32)
                padded[s, pl.ds(place, depth), :] = given[s][lag]
            lane = pl.multiple_of(group * LANES, LANES)
            left = jnp.concatenate([kernel_ref[part * lags + lag, :, pl.ds(lane, tall)] for lag in range(lags)], axis=1)
            product = jnp.dot(left, padded[s], preferred_element_type=jnp.float32)
            if s or seed is not None:
                product = (total if s else seed_ref)[...] + product
            total[...] = product
        if incident is not None:
            height = incident.shape[0]
            mine = pl.ds(pl.multiple_of(chosen_ref[0] * height, height), height)
            total[mine, :] = total[mine, :] - incident_ref[...]
        if spread:
            turned[...] = total[...].T
            width = columns // spread
            for m in range(spread):
                at = pl.multiple_of((row ^ m) * width, width)
                value = turned[pl.ds(at, width), :]
                if m % 2:
                    give[m // 2][...] = value
                else:
                    keep[m // 2] = value

    whole = (rows, columns)
    scratch = [pltpu.VMEM((count, lags * tall, columns), kernels.dtype)]
    if spread:
        piece = (columns // spread, rows)
        out_shape = [jax.ShapeDtypeStruct((spread // 2, *piece), jnp.float32)]
        out_shape += [jax.ShapeDtypeStruct(piece, jnp.float32)] * (spread // 2)
        scratch += [pltpu.VMEM(whole, jnp.float32), pltpu.VMEM(whole[::-1], jnp.float32)]
    else:
        out_shape = jax.ShapeDtypeStruct(whole, jnp.float32)
    in_specs = [VMEM] * (1 + count + len(extra))
    if incident is not None:
        in_specs[-1] = SMEM

    return pl.pallas_call(
        body,
        out_shape=out_shape,
        in_specs=in_specs,
        out_specs=[VMEM] * len(out_shape) if spread else VMEM,
        scratch_shapes=scratch,
        compiler_params=params(16 if rows <= 512 else 40),
        cost_estimate=cost(2 * count * lags * rows * tall * columns, 2 * count * lags * tall * (rows + columns)),
        name="multiply",
    )(kernels, *[block[3] for block in blocks], *extra)


def steady(dense, driven, density, rounded, near_side, chosen):
    width, rows = driven.shape

    def body(*refs):
        dense_ref, driven_ref, density_ref, rounded_ref = refs[:4]
        out_ref = refs[-1]

        def term(ref, k):
            return lax.dot_general(
                ref[...],
                dense_ref[:, k * rows : (k + 1) * rows],
                (((1,), (1,)), ((), ())),
                preferred_element_type=jnp.float32,
            )

        near = term(rounded_ref, 1)
        if near_side is not None:
            near = near + term(refs[4], 2)
        old = density_ref[...]
        out_ref[...] = old + damping * (driven_ref[...] - old - near)
        if last:
            count = chosen.shape[0]
            height = rows // count
            for m in range(count):
                at = pl.multiple_of(refs[5][m] * height, height)
                refs[6][:, m * height : (m + 1) * height] = out_ref[:, pl.ds(at, height)]

    last = chosen is not None
    sides = [] if near_side is None else [near_side]
    whole = (width, rows)
    return pl.pallas_call(
        body,
        out_shape=jax.ShapeDtypeStruct(whole, jnp.float32),
        in_specs=[VMEM] * (4 + len(sides)) + [SMEM] * last,
        out_specs=VMEM,
        scratch_shapes=[pltpu.VMEM(whole, jnp.float32)] * last,
        compiler_params=params(8 if rows <= 512 else 24),
        cost_estimate=cost(4 * width * rows * rows, 4 * rows * rows + 16 * width * rows),
        name="steady",
    )(dense, driven, density, rounded, *sides, *([chosen] if last else []))


def sweep(dense, base, far_side, near_side, pieces):
    width, rows = base.shape

    sides = [(far_side, 0)] + ([] if near_side is None else [(near_side, 2)])

    def body(dense_ref, base_ref, *refs):
        side_refs, outs = refs[: len(sides)], refs[len(sides) :]
        near = sum(
            lax.dot_general(
                ref[...],
                dense_ref[:, k * rows : (k + 1) * rows],
                (((1,), (1,)), ((), ())),
                preferred_element_type=jnp.float32,
            )
            for ref, (_, k) in zip(side_refs, sides)
        )
        new = base_ref[...] - damping * near
        if pieces:
            height = rows // pieces
            for m in range(pieces):
                outs[m][...] = new[:, m * height : (m + 1) * height]
        else:
            outs[0][...] = new
            outs[1][...] = new.astype(far_side.dtype)

    if pieces:
        out_shape = [jax.ShapeDtypeStruct((width, rows // pieces), jnp.float32)] * pieces
    else:
        out_shape = [jax.ShapeDtypeStruct((width, rows), kind) for kind in (jnp.float32, far_side.dtype)]
    return pl.pallas_call(
        body,
        out_shape=out_shape,
        in_specs=[VMEM] * (2 + len(sides)),
        out_specs=[VMEM] * len(out_shape),
        compiler_params=params(8 if rows <= 512 else 24),
        cost_estimate=cost(2 * width * rows * rows, 2 * rows * rows + 12 * width * rows),
        name="sweep",
    )(dense, base, *[side for side, _ in sides])


def assemble(pieces):
    width, height = pieces[0].shape
    columns = width * len(pieces)

    def body(*refs):
        row = lax.axis_index("row")
        out_ref, turned = refs[-2:]
        for m in range(len(pieces)):
            at = pl.multiple_of((row ^ m) * width, width)
            turned[pl.ds(at, width), :] = refs[m][...]
        out_ref[0] = turned[...].T

    return pl.pallas_call(
        body,
        out_shape=jax.ShapeDtypeStruct((1, height, columns), jnp.float32),
        in_specs=[VMEM] * len(pieces),
        out_specs=VMEM,
        scratch_shapes=[pltpu.VMEM((columns, height), jnp.float32)],
        compiler_params=params(8),
        cost_estimate=cost(0, 8 * columns * height),
        name="assemble",
    )(*pieces)


def per_device(kernels, history, incident, owner, tile_pairs, tile_values, tile_counts):
    row_count = lax.axis_size("row")
    col_count = lax.axis_size("col")
    lags, _, _ = history.shape
    half = lags // PARTS

    def across_rows(x, m):
        return lax.ppermute(x, "row", [(i, i ^ m) for i in range(row_count)])

    walk = list(range(0, col_count, 2)) + list(range(col_count - 1, 0, -2))

    def swap_walk(x, side):
        return lax.ppermute(x, "col", [(walk[p], walk[mate(p, side, col_count)]) for p in range(col_count)])

    def swap_cols(x, side):
        return lax.ppermute(x, "col", [(c, mate(c, side, col_count)) for c in range(col_count)])

    chosen, own_tiles = prepare(owner, tile_pairs.T, tile_counts, tile_values)
    parts = [own_tiles]
    for m in range(1, row_count):
        parts.append(across_rows(own_tiles, m))
    dense, dense_last = stack_rows(chosen, parts)

    halves = [history[i * half : (i + 1) * half] for i in range(PARTS)]
    moving = {(side, i): halves[i] for i in range(PARTS) for side in (1, 2)}
    final = col_count // 2

    def turn(step, rank):
        out = {}
        for i in range(PARTS):
            side = early_side(step, i, final) if rank == 0 else 3 - early_side(step, i, final)
            out[side, i] = swap_walk(moving[3 - side, i], side)
        return out

    def over_rows(keep, give, kind):
        bit = 1
        odd = list(give)
        even = [keep[t] for t in range(row_count // 2)]
        lost = []
        while True:
            got = []
            for t, x in enumerate(odd):
                near = x
                if bit > 1 and kind != x.dtype:
                    near = lax.reduce_precision(x, jnp.finfo(kind).nexp, jnp.finfo(kind).nmant)
                    lost.append(((2 * t + 1) * bit, (x - near).astype(kind)))
                got.append(across_rows(near.astype(kind if bit > 1 else x.dtype), bit).astype(x.dtype))
            summed = [x + y for x, y in zip(even, got)]
            if len(summed) == 1:
                return summed[0], lost
            bit *= 2
            even, odd = summed[0::2], summed[1::2]

    total = multiply(kernels, [(0, 1, i, x) for i, x in enumerate(halves)], None, None, None, 0)
    for step in range(1, final):
        turns = [turn(step, rank) for rank in range(2)]
        moving = turns[0] | turns[1]
        for rank in range(2):
            blocks = [(step, side, i, x) for (side, i), x in turns[rank].items()]
            early = (step, rank) == (final - 1, 0)
            field = (incident[0], chosen) if early else (None, None)
            total = multiply(kernels, blocks, total, *field, row_count if early else 0)
            if early:
                early_sum, _ = over_rows(total[0], total[1:], jnp.float32)
                total = None
    for i, ((_, part), x) in enumerate(reversed(turn(final, 0).items())):
        total = multiply(kernels, [(final, 1, part, x)], total, None, None, i * row_count)
    late_sum, lost = over_rows(total[0], total[1:], jnp.bfloat16)
    driven = -(late_sum + early_sum)

    density = driven
    rounded = density.astype(jnp.bfloat16)
    for step in range(SWEEPS):
        far_side = swap_cols(rounded, 2)
        near_side = swap_cols(rounded, 1)
        last = step == SWEEPS - 1
        if step == 0:
            rest = sum(across_rows(x, m).astype(jnp.float32) for m, x in lost)
        if step == 1:
            driven, density = driven - rest, density - rest
        early_side_only, late_side = (None, near_side) if step == 0 else (near_side, None)
        base = steady(dense, driven, density, rounded, early_side_only, chosen if last else None)
        result = sweep(dense_last if last else dense, base, far_side, late_side, row_count if last else 0)
        if step < SWEEPS - 1:
            density, rounded = result

    pieces = [result[0]]
    for m in range(1, row_count):
        pieces.append(across_rows(result[m], m))
    return assemble(pieces)


def solution(mesh):
    in_specs = (
        P(None, "col", "row"),
        P(None, ("row", "col"), None),
        P(("row", "col"), None, None),
        P(),
        P(("row", "col"), None),
        P(("row", "col"), None, None),
        P(("row", "col")),
    )
    out_specs = P(("row", "col"), None, None)
    return jax.shard_map(
        per_device, mesh=mesh, in_specs=in_specs, out_specs=out_specs, check_vma=False
    )
```

```python
import math

import jax
import jax.numpy as jnp
from jax import lax
from jax.experimental import pallas as pl
from jax.experimental.pallas import tpu as pltpu
from jax.sharding import PartitionSpec as P


SWEEPS = 3
PARTS = 2
LANES = 128


damping = 0.7


def cost(flops, moved):
    return pl.CostEstimate(flops=flops, bytes_accessed=moved, transcendentals=0)


def params(limit):
    return pltpu.CompilerParams(vmem_limit_bytes=limit * 2**20)


VMEM = pl.BlockSpec(memory_space=pltpu.VMEM)
SMEM = pl.BlockSpec(memory_space=pltpu.SMEM)


def mate(p, side, count):
    return p ^ 1 if side == 1 else (p + (1 if p % 2 else -1)) % count


def early_side(step, part, final):
    return 1 if (final - step + part) % 2 == 0 else 2


def prepare(owner, pairs, counts, tile_values):
    rows = lax.axis_size("row")
    cols = lax.axis_size("col")
    tiles, height, deep = tile_values.shape
    slots = 3 * rows

    def body(owner_ref, pairs_ref, counts_ref, tile_ref, chosen_ref, out_ref, pick, live):
        row, col = lax.axis_index("row"), lax.axis_index("col")
        for i in range(rows):
            chosen_ref[owner_ref[col * rows + i] ^ row] = i
        for q in range(slots):
            pick[q] = 0
            live[q] = 0
        ahead = jnp.where(lax.rem(col, 2) == 0, 1, cols - 1)
        for t in range(tiles):

            @pl.when(t < counts_ref[0])
            def _(t=t):
                source = pairs_ref[1, t]
                apart = lax.rem(source // rows - col + cols, cols)
                block = jnp.where(apart == 0, 1, jnp.where(apart == ahead, 2, 0))
                slot = block * rows + lax.rem(source, rows)
                pick[slot] = t
                live[slot] = 1

        for q in range(slots):
            tile = tile_ref[pick[q]]
            out_ref[:, q * deep : (q + 1) * deep] = jnp.where(live[q] > 0, tile, jnp.zeros_like(tile))

    return pl.pallas_call(
        body,
        out_shape=[
            jax.ShapeDtypeStruct((rows,), jnp.int32),
            jax.ShapeDtypeStruct((height, slots * deep), tile_values.dtype),
        ],
        in_specs=[SMEM] * 3 + [VMEM],
        out_specs=[SMEM, VMEM],
        scratch_shapes=[pltpu.SMEM((slots,), jnp.int32), pltpu.SMEM((slots,), jnp.int32)],
        compiler_params=params(4),
        cost_estimate=cost(0, 4 * slots * height * deep),
        name="prepare",
    )(owner, pairs, counts, tile_values)


def stack_rows(chosen, parts):
    count = len(parts)
    rows, width = parts[0].shape
    side = width // 3

    def body(chosen_ref, *refs):
        for m in range(count):
            at = pl.multiple_of(chosen_ref[m] * rows, rows)
            refs[-2][pl.ds(at, rows), :] = refs[m][...]
            refs[-1][m * rows : (m + 1) * rows, :] = refs[m][:, :side]

    return pl.pallas_call(
        body,
        out_shape=[
            jax.ShapeDtypeStruct((count * rows, width), parts[0].dtype),
            jax.ShapeDtypeStruct((count * rows, side), parts[0].dtype),
        ],
        in_specs=[SMEM] + [VMEM] * count,
        out_specs=[VMEM] * 2,
        compiler_params=params(4 if rows * count <= 512 else 24),
        cost_estimate=cost(0, 4 * count * rows * width),
        name="stack_rows",
    )(chosen, *parts)


def multiply(kernels, blocks, seed, incident, chosen, spread):
    rows = kernels.shape[1]
    cols = lax.axis_size("col")
    count = len(blocks)
    lags, depth, columns = blocks[0][3].shape
    tall = -(-(depth + LANES - math.gcd(depth, LANES)) // LANES) * LANES
    extra = ([] if seed is None else [seed]) + ([] if incident is None else [incident, chosen])

    def body(kernel_ref, *refs):
        given, refs = refs[:count], refs[count:]
        seed_ref, refs = (None, refs) if seed is None else (refs[0], refs[1:])
        if incident is not None:
            (incident_ref, chosen_ref), refs = refs[:2], refs[2:]
        if spread:
            keep, give, (padded, total, turned) = refs[0], refs[1:-3], refs[-3:]
        else:
            total, padded = refs
        row, col = lax.axis_index("row"), lax.axis_index("col")
        stop = jnp.where(lax.rem(col, 2) == 0, col // 2, cols - 1 - col // 2)
        sign = jnp.where(lax.rem(stop, 2) == 1, 1, -1)
        padded[...] = jnp.zeros_like(padded)
        for s, (step, side, part, _) in enumerate(blocks):
            back = sign * (step if side == 1 else -step)
            at = lax.rem(stop - back + cols, cols)
            source = jnp.where(at < cols // 2, 2 * at, 2 * (cols - 1 - at) + 1)
            group = jnp.minimum(source * depth // LANES, (kernels.shape[2] - tall) // LANES)
            shift = source * depth - group * LANES
            for lag in range(lags):
                place = pl.multiple_of(lag * tall + shift, 32)
                padded[s, pl.ds(place, depth), :] = given[s][lag]
            lane = pl.multiple_of(group * LANES, LANES)
            left = jnp.concatenate([kernel_ref[part * lags + lag, :, pl.ds(lane, tall)] for lag in range(lags)], axis=1)
            product = jnp.dot(left, padded[s], preferred_element_type=jnp.float32)
            if s or seed is not None:
                product = (total if s else seed_ref)[...] + product
            total[...] = product
        if incident is not None:
            height = incident.shape[0]
            mine = pl.ds(pl.multiple_of(chosen_ref[0] * height, height), height)
            total[mine, :] = total[mine, :] - incident_ref[...]
        if spread:
            turned[...] = total[...].T
            width = columns // spread
            for m in range(spread):
                at = pl.multiple_of((row ^ m) * width, width)
                value = turned[pl.ds(at, width), :]
                if m % 2:
                    give[m // 2][...] = value
                else:
                    keep[m // 2] = value

    whole = (rows, columns)
    scratch = [pltpu.VMEM((count, lags * tall, columns), kernels.dtype)]
    if spread:
        piece = (columns // spread, rows)
        out_shape = [jax.ShapeDtypeStruct((spread // 2, *piece), jnp.float32)]
        out_shape += [jax.ShapeDtypeStruct(piece, jnp.float32)] * (spread // 2)
        scratch += [pltpu.VMEM(whole, jnp.float32), pltpu.VMEM(whole[::-1], jnp.float32)]
    else:
        out_shape = jax.ShapeDtypeStruct(whole, jnp.float32)
    in_specs = [VMEM] * (1 + count + len(extra))
    if incident is not None:
        in_specs[-1] = SMEM

    return pl.pallas_call(
        body,
        out_shape=out_shape,
        in_specs=in_specs,
        out_specs=[VMEM] * len(out_shape) if spread else VMEM,
        scratch_shapes=scratch,
        compiler_params=params(16 if rows <= 512 else 40),
        cost_estimate=cost(2 * count * lags * rows * tall * columns, 2 * count * lags * tall * (rows + columns)),
        name="multiply",
    )(kernels, *[block[3] for block in blocks], *extra)


def steady(dense, driven, density, rounded, near_side, chosen):
    width, rows = driven.shape

    def body(*refs):
        dense_ref, driven_ref, density_ref, rounded_ref = refs[:4]
        out_ref = refs[-1]

        def term(ref, k):
            return lax.dot_general(
                ref[...],
                dense_ref[:, k * rows : (k + 1) * rows],
                (((1,), (1,)), ((), ())),
                preferred_element_type=jnp.float32,
            )

        near = term(rounded_ref, 1)
        if near_side is not None:
            near = near + term(refs[4], 2)
        old = density_ref[...]
        out_ref[...] = old + damping * (driven_ref[...] - old - near)
        if last:
            count = chosen.shape[0]
            height = rows // count
            for m in range(count):
                at = pl.multiple_of(refs[5][m] * height, height)
                refs[6][:, m * height : (m + 1) * height] = out_ref[:, pl.ds(at, height)]

    last = chosen is not None
    sides = [] if near_side is None else [near_side]
    whole = (width, rows)
    return pl.pallas_call(
        body,
        out_shape=jax.ShapeDtypeStruct(whole, jnp.float32),
        in_specs=[VMEM] * (4 + len(sides)) + [SMEM] * last,
        out_specs=VMEM,
        scratch_shapes=[pltpu.VMEM(whole, jnp.float32)] * last,
        compiler_params=params(8 if rows <= 512 else 24),
        cost_estimate=cost(4 * width * rows * rows, 4 * rows * rows + 16 * width * rows),
        name="steady",
    )(dense, driven, density, rounded, *sides, *([chosen] if last else []))


def sweep(dense, base, far_side, near_side, pieces):
    width, rows = base.shape

    sides = [(far_side, 0)] + ([] if near_side is None else [(near_side, 2)])

    def body(dense_ref, base_ref, *refs):
        side_refs, outs = refs[: len(sides)], refs[len(sides) :]
        near = sum(
            lax.dot_general(
                ref[...],
                dense_ref[:, k * rows : (k + 1) * rows],
                (((1,), (1,)), ((), ())),
                preferred_element_type=jnp.float32,
            )
            for ref, (_, k) in zip(side_refs, sides)
        )
        new = base_ref[...] - damping * near
        if pieces:
            height = rows // pieces
            for m in range(pieces):
                outs[m][...] = new[:, m * height : (m + 1) * height]
        else:
            outs[0][...] = new
            outs[1][...] = new.astype(far_side.dtype)

    if pieces:
        out_shape = [jax.ShapeDtypeStruct((width, rows // pieces), jnp.float32)] * pieces
    else:
        out_shape = [jax.ShapeDtypeStruct((width, rows), kind) for kind in (jnp.float32, far_side.dtype)]
    return pl.pallas_call(
        body,
        out_shape=out_shape,
        in_specs=[VMEM] * (2 + len(sides)),
        out_specs=[VMEM] * len(out_shape),
        compiler_params=params(8 if rows <= 512 else 24),
        cost_estimate=cost(2 * width * rows * rows, 2 * rows * rows + 12 * width * rows),
        name="sweep",
    )(dense, base, *[side for side, _ in sides])


def assemble(pieces):
    width, height = pieces[0].shape
    columns = width * len(pieces)

    def body(*refs):
        row = lax.axis_index("row")
        out_ref, turned = refs[-2:]
        for m in range(len(pieces)):
            at = pl.multiple_of((row ^ m) * width, width)
            turned[pl.ds(at, width), :] = refs[m][...]
        out_ref[0] = turned[...].T

    return pl.pallas_call(
        body,
        out_shape=jax.ShapeDtypeStruct((1, height, columns), jnp.float32),
        in_specs=[VMEM] * len(pieces),
        out_specs=VMEM,
        scratch_shapes=[pltpu.VMEM((columns, height), jnp.float32)],
        compiler_params=params(8),
        cost_estimate=cost(0, 8 * columns * height),
        name="assemble",
    )(*pieces)


def per_device(kernels, history, incident, owner, tile_pairs, tile_values, tile_counts):
    row_count = lax.axis_size("row")
    col_count = lax.axis_size("col")
    lags, _, _ = history.shape
    half = lags // PARTS

    def across_rows(x, m):
        return lax.ppermute(x, "row", [(i, i ^ m) for i in range(row_count)])

    walk = list(range(0, col_count, 2)) + list(range(col_count - 1, 0, -2))

    def swap_walk(x, side):
        return lax.ppermute(x, "col", [(walk[p], walk[mate(p, side, col_count)]) for p in range(col_count)])

    def swap_cols(x, side):
        return lax.ppermute(x, "col", [(c, mate(c, side, col_count)) for c in range(col_count)])

    chosen, own_tiles = prepare(owner, tile_pairs.T, tile_counts, tile_values)
    parts = [own_tiles]
    for m in range(1, row_count):
        parts.append(across_rows(own_tiles, m))
    dense, dense_last = stack_rows(chosen, parts)

    halves = [history[i * half : (i + 1) * half] for i in range(PARTS)]
    moving = {(side, i): halves[i] for i in range(PARTS) for side in (1, 2)}
    final = col_count // 2

    def turn(step, rank):
        out = {}
        for i in range(PARTS):
            side = early_side(step, i, final) if rank == 0 else 3 - early_side(step, i, final)
            out[side, i] = swap_walk(moving[3 - side, i], side)
        return out

    def over_rows(keep, give, kind):
        bit = 1
        odd = list(give)
        even = [keep[t] for t in range(row_count // 2)]
        lost = []
        while True:
            got = []
            for t, x in enumerate(odd):
                near = x
                if kind != x.dtype:
                    near = lax.reduce_precision(x, jnp.finfo(kind).nexp, jnp.finfo(kind).nmant)
                    lost.append(((2 * t + 1) * bit, (x - near).astype(kind)))
                got.append(across_rows(near.astype(kind), bit).astype(x.dtype))
            summed = [x + y for x, y in zip(even, got)]
            if len(summed) == 1:
                return summed[0], lost
            bit *= 2
            even, odd = summed[0::2], summed[1::2]

    total = multiply(kernels, [(0, 1, i, x) for i, x in enumerate(halves)], None, None, None, 0)
    for step in range(1, final):
        turns = [turn(step, rank) for rank in range(2)]
        moving = turns[0] | turns[1]
        for rank in range(2):
            blocks = [(step, side, i, x) for (side, i), x in turns[rank].items()]
            early = (step, rank) == (final - 1, 1)
            field = (incident[0], chosen) if early else (None, None)
            total = multiply(kernels, blocks, total, *field, row_count if early else 0)
            if early:
                early_sum, _ = over_rows(total[0], total[1:], jnp.float32)
                total = None
    for i, ((_, part), x) in enumerate(reversed(turn(final, 0).items())):
        total = multiply(kernels, [(final, 1, part, x)], total, None, None, i * row_count)
    late_sum, lost = over_rows(total[0], total[1:], jnp.bfloat16)
    driven = -(late_sum + early_sum)

    density = driven
    rounded = density.astype(jnp.bfloat16)
    for step in range(SWEEPS):
        far_side = swap_cols(rounded, 2)
        near_side = swap_cols(rounded, 1)
        last = step == SWEEPS - 1
        if step == 0:
            rest = sum(across_rows(x, m).astype(jnp.float32) for m, x in lost)
        if step == 1:
            driven, density = driven - rest, density - rest
        early_side_only, late_side = (None, near_side) if step == 0 else (near_side, None)
        base = steady(dense, driven, density, rounded, early_side_only, chosen if last else None)
        result = sweep(dense_last if last else dense, base, far_side, late_side, row_count if last else 0)
        if step < SWEEPS - 1:
            density, rounded = result

    pieces = [result[0]]
    for m in range(1, row_count):
        pieces.append(across_rows(result[m], m))
    return assemble(pieces)


def solution(mesh):
    in_specs = (
        P(None, "col", "row"),
        P(None, ("row", "col"), None),
        P(("row", "col"), None, None),
        P(),
        P(("row", "col"), None),
        P(("row", "col"), None, None),
        P(("row", "col")),
    )
    out_specs = P(("row", "col"), None, None)
    return jax.shard_map(
        per_device, mesh=mesh, in_specs=in_specs, out_specs=out_specs, check_vma=False
    )
```
